512 devices in a mesh: mem: 32 (over z, core), lat: 16 (over x, y).
Axes of the slice: x: 4, y: 4, z: 16, core: 2. Of those that a mesh axis runs over, the one named last changes fastest.
Arguments:
- equivalents: float32 [384, 393216], P('mem', 'lat'), may hold values from -12 to 12
- innovations: float32 [384, 393216], P('mem', 'lat'), may hold values from -6 to 6
- obs_var: float32 [393216], P('lat'), may hold values from 0.5 to 2
- taper_tiles: bfloat16 [2, 512, 512], replicated, may hold values from 0 to 1
- region_blocks: int32 [16, 32], replicated, may hold values from 1 to 2, 48 in all within a row
- pair_mask: int32 [16, 48], replicated, may hold values 0 or 1
- taper_index: int32 [16, 48, 3], replicated, may hold values from 0 to 1
- eig_low: float32 [1], replicated, may hold values from 0.3 to 0.6
- eig_high: float32 [1], replicated, may hold values from 6 to 10
Outputs:
- solution: float32 [384, 393216], P('mem', 'lat')
The draws below stay inside these ranges and needn't reach their ends.
Inputs may be any that keep to these rules, and one draw needn't show every extreme that they name: `region_blocks`: in every band the counts sum to 48 and some region holds exactly 2 blocks.
All inputs are finite; a program needn't handle non-finite values.
Results may differ from the reference program's by a relative error of at most 0.0044.
Values may be sent and summed in bfloat16 or wider, within the bound.
A program may use at most 64 MiB of HBM per device.

```python
import math
import jax
import jax.numpy as jnp
import numpy as np
from jax import lax

M = 384
BLOCK = 512
MAXB = 2
N_TAPER = 2
ITERS = 3
BAND_BLOCKS = 48
NOBS = 393216
N_MEM = 32
N_LAT = 16


def draw_equivalents(key, part):
    base_key = jax.random.fold_in(key, 4711)
    key_back, key_noise = jax.random.split(base_key, 2)
    background = 4.0 * jax.random.normal(key_back, (1, NOBS), jnp.float32)
    noise = jax.random.normal(key_noise, (M, NOBS), jnp.float32)
    return jnp.clip(background + noise, -12.0, 12.0).astype(jnp.float32)


def touch_ends(entries, stream_key, least, largest):
    longest = entries.shape.index(max(entries.shape))
    spots = []
    for shift in (0, 1):
        where = [jax.random.randint(jax.random.fold_in(stream_key, axis), (), 0, length) for axis, length in enumerate(entries.shape)]
        where[longest] = (where[longest] + shift) % entries.shape[longest]
        spots.append(tuple(where))
    return entries.at[spots[0]].set(least).at[spots[1]].set(largest)


def levels(rng, dims, pieces, smallest, high):
    gain = 1.0
    for position, shards_of in pieces:
        steps = jax.random.uniform(jax.random.fold_in(jax.random.fold_in(rng, 6), position), (shards_of,), jnp.float32, smallest / len(pieces), high / len(pieces))
        gain = gain * jnp.repeat(jnp.exp(steps), dims[position] // shards_of).reshape((-1,) + (1,) * (len(dims) - 1 - position))
    return gain


def length_profile(amount, total, limit, slope):
    loads = [(1 << 20) // math.isqrt(standing ** slope) + 1 for standing in range(2, amount + 1)]
    spare, given = total - limit - (amount - 1), [1] * (amount - 1)
    while spare > 0:
        free = [i for i in range(amount - 1) if given[i] < limit]
        mass, left = sum([loads[i] for i in free]), spare
        for i in free:
            extra = min(limit - given[i], max(1, left * loads[i] // mass), spare)
            given[i] = given[i] + extra
            spare = spare - extra
    return np.array([limit] + given)


def ragged(stream_key, count, total, bound, skew):
    if count == 2:
        one = jax.random.randint(stream_key, (), max(1, total - bound), min(bound, total - 1) + 1)
        return jnp.stack([one, total - one])
    lengths = jnp.asarray(length_profile(count, total, bound, skew), jnp.int32)
    couples = (count - 1) // 2
    source_of, receiver = lengths[1:1 + 2 * couples:2], lengths[2:2 + 2 * couples:2]
    slack = jnp.minimum(source_of - 1, bound - receiver)
    passed = jax.random.randint(jax.random.fold_in(stream_key, 1), (couples,), 0, 1 << 20) % (slack + 1)
    lengths = lengths.at[1:1 + 2 * couples:2].set(source_of - passed).at[2:2 + 2 * couples:2].set(receiver + passed)
    return lengths[jax.random.permutation(jax.random.fold_in(stream_key, 2), count)]


def centred(own_key, shape, spread, reach, pieces=(), kind=jnp.bfloat16):
    values = spread * jax.random.normal(own_key, shape, jnp.float32)
    if pieces:
        values = values * levels(own_key, shape, pieces, -0.22, 0.18)
    return jnp.clip(values, -reach, reach).astype(kind)


def setup_inputs(seed: int = 0) -> dict:
    seeds = jax.random.split(jax.random.key(seed), 10)
    return {
        "equivalents": draw_equivalents(jax.random.fold_in(seeds[9], 71), 0),
        "innovations": centred(seeds[1], (M, NOBS), 1.0, 6.0, ((0, 32), (1, 16)), jnp.float32),
        "obs_var": jnp.clip(jnp.exp(math.log(2.0) - 1.3862944 * jax.random.uniform(seeds[2], (NOBS,), jnp.float32) ** levels(seeds[2], (NOBS,), ((0, 16),), -0.2, 0.2)), 0.5, 2.0),
        "taper_tiles": jnp.clip(jax.random.uniform(seeds[3], (N_TAPER, BLOCK, BLOCK), jnp.float32, 0.0, 1.0), 0.0, 1.0).astype(jnp.bfloat16),
        "region_blocks": jax.vmap(lambda own: ragged(own, N_MEM, BAND_BLOCKS, MAXB, 2))(jax.random.split(seeds[4], N_LAT)).reshape((N_LAT, N_MEM)).astype(jnp.int32),
        "pair_mask": touch_ends((jax.random.randint(seeds[5], (N_LAT, BAND_BLOCKS), 0, 4) < 3).astype(jnp.int32), jax.random.fold_in(seeds[5], 1), 0, 1),
        "taper_index": touch_ends(jax.random.randint(seeds[6], (N_LAT, BAND_BLOCKS, 3), 0, N_TAPER), jax.random.fold_in(seeds[6], 1), 0, N_TAPER - 1).astype(jnp.int32),
        "eig_low": jnp.clip(jax.random.uniform(seeds[7], (1,), jnp.float32, 0.3, 0.6), 0.3, 0.6),
        "eig_high": jnp.clip(jax.random.uniform(seeds[8], (1,), jnp.float32, 6.0, 10.0), 6.0, 10.0),
    }


exact_precision = lax.Precision.HIGHEST


def exclusive_starts(counts):
    return (jnp.cumsum(counts, axis=1) - counts).astype(jnp.int32)


def reference(equivalents, innovations, obs_var, taper_tiles, region_blocks, pair_mask, taper_index, eig_low, eig_high):
    inv_scale = (M - 1) ** -0.5
    ens_blocks = equivalents.T.reshape(N_LAT, BAND_BLOCKS, BLOCK, M)
    mean_rows = jnp.mean(ens_blocks, axis=3, keepdims=True)
    perturb = ((ens_blocks - mean_rows) * inv_scale).astype(jnp.bfloat16)
    starts = exclusive_starts(region_blocks)
    positions = jnp.arange(BAND_BLOCKS, dtype=jnp.int32)
    is_start = jnp.any(positions[None, :, None] == starts[:, None, :], axis=2)
    next_start = jnp.concatenate([is_start[:, 1:], jnp.ones((N_LAT, 1), dtype=jnp.bool_)], axis=1)
    active = ((pair_mask == 1) & jnp.logical_not(next_start)).astype(jnp.float32)
    taper_table = taper_tiles.astype(jnp.float32)

    def band_cov(inputs):
        pert_band, index_band, active_band = inputs
        pert_f32 = pert_band.astype(jnp.float32)
        following = jnp.concatenate([pert_f32[1:], jnp.zeros_like(pert_f32[:1])], axis=0)
        tile_self = taper_table[index_band[:, 0]]
        tile_self = 0.5 * (tile_self + jnp.swapaxes(tile_self, 1, 2))
        prod_self = jnp.einsum("kim,kjm->kij", pert_f32, pert_f32, precision=exact_precision)
        cov_self = (tile_self * prod_self).astype(jnp.bfloat16)
        tile_east = taper_table[index_band[:, 1]]
        prod_east = jnp.einsum("kim,kjm->kij", pert_f32, following, precision=exact_precision)
        cov_east = (tile_east * prod_east * active_band[:, None, None]).astype(jnp.bfloat16)
        return cov_self, cov_east

    cov_self, cov_east = lax.map(band_cov, (perturb, taper_index, active))
    band_rows = jnp.arange(N_LAT, dtype=jnp.int32)[:, None]
    first_pert = perturb[band_rows, starts]
    north_index = taper_index[band_rows, starts, 2]

    def north_cov(inputs):
        lower_first, upper_first, index_row = inputs
        product = jnp.einsum("nim,njm->nij", lower_first.astype(jnp.float32), upper_first.astype(jnp.float32), precision=exact_precision)
        return (taper_table[index_row] * product).astype(jnp.bfloat16)

    cov_north = lax.map(north_cov, (first_pert[:-1], first_pert[1:], north_index[:-1]))
    variance = obs_var.reshape(N_LAT, BAND_BLOCKS, BLOCK, 1)

    def band_apply(inputs):
        self_blocks, east_blocks, dir_band = inputs
        dir_f32 = dir_band.astype(jnp.float32)
        following = jnp.concatenate([dir_f32[1:], jnp.zeros_like(dir_f32[:1])], axis=0)
        before = jnp.concatenate([jnp.zeros_like(dir_f32[:1]), dir_f32[:-1]], axis=0)
        east_f32 = east_blocks.astype(jnp.float32)
        east_prev = jnp.concatenate([jnp.zeros_like(east_f32[:1]), east_f32[:-1]], axis=0)
        summed = jnp.einsum("kij,kjm->kim", self_blocks.astype(jnp.float32), dir_f32, precision=exact_precision)
        summed = summed + jnp.einsum("kij,kjm->kim", east_f32, following, precision=exact_precision)
        return summed + jnp.einsum("kji,kjm->kim", east_prev, before, precision=exact_precision)

    def edge_apply(inputs):
        cov_block, lower_first, upper_first = inputs
        cov_f32 = cov_block.astype(jnp.float32)
        upward = jnp.einsum("nij,njm->nim", cov_f32, upper_first, precision=exact_precision)
        downward = jnp.einsum("nji,njm->nim", cov_f32, lower_first, precision=exact_precision)
        return upward, downward

    def operate(direction):
        dir_bf = direction.astype(jnp.bfloat16)
        result = variance * direction + lax.map(band_apply, (cov_self, cov_east, dir_bf))
        first_dir = dir_bf[band_rows, starts].astype(jnp.float32)
        upward, downward = lax.map(edge_apply, (cov_north, first_dir[:-1], first_dir[1:]))
        zero_band = jnp.zeros_like(upward[:1])
        edge_sum = jnp.concatenate([upward, zero_band], axis=0) + jnp.concatenate([zero_band, downward], axis=0)
        return result.at[band_rows, starts].add(edge_sum)

    low_bound = eig_low[0]
    high_bound = eig_high[0]
    centre = 0.5 * (high_bound + low_bound)
    half_width = 0.5 * (high_bound - low_bound)
    ratio_scale = centre / half_width
    ratio_prev = 1.0 / ratio_scale
    residual = innovations.T.reshape(N_LAT, BAND_BLOCKS, BLOCK, M)
    solution = jnp.zeros_like(residual)
    direction = residual / centre
    for iteration in range(ITERS):
        solution = solution + direction
        if iteration + 1 < ITERS:
            residual = residual - operate(direction)
            ratio_next = 1.0 / (2.0 * ratio_scale - ratio_prev)
            direction = ratio_next * ratio_prev * direction + (2.0 * ratio_next / half_width) * residual
            ratio_prev = ratio_next
    return solution.reshape(N_LAT * BAND_BLOCKS * BLOCK, M).T
```

```python
import jax
import jax.numpy as jnp
from jax import lax
from jax.experimental import pallas as pl
from jax.experimental.pallas import tpu as pltpu
from jax.sharding import PartitionSpec as P

M = 384
BLOCK = 512
BAND = 48
GROUPS = 4
BF = jnp.bfloat16
F32 = jnp.float32
MESH = pl.DeviceIdType.MESH
VM = pl.BlockSpec(memory_space=pltpu.VMEM)
HB = pl.BlockSpec(memory_space=pl.ANY)
SM = pl.BlockSpec(memory_space=pltpu.SMEM)
INV = (M - 1) ** -0.5


def coefficients(lo, hi):
    low = jnp.full((1, BLOCK), lo, F32)
    high = jnp.full((1, BLOCK), hi, F32)
    centre = 0.5 * (high + low)
    half = 0.5 * (high - low)
    scale = centre / half
    q0 = 1.0 / scale
    q1 = 1.0 / (2.0 * scale - q0)
    q2 = 1.0 / (2.0 * scale - q1)
    return centre, q1 * q0, 2.0 * q1 / half, q2 * q1, 2.0 * q2 / half


def fill_starts(region_ref, band, starts):
    def step(m, total):
        starts[m] = total
        return total + region_ref[band, m]

    lax.fori_loop(0, 32, step, jnp.int32(0))


def peer_of(i, z, c):
    t = i // 2
    odd = t % 2
    dz = (8 - (t + 1) // 2) * (2 * odd - 1)
    return (z + dz + 16) % 16 * 2 + (c + 1 - i % 2) % 2


def mirror(i):
    t = i // 2
    return i + 4 * (t % 2) - 2


ROOT = 12.0**0.5


def pack_kernel(
    eq_hbm, inn_hbm, var_hbm, index_hbm, region_ref, mask_ref, lo_ref, hi_ref,
    send_p, send_low, send_r, var_out, pick,
    eq, inn, rows_here, rows_low, starts, low_starts, sem,
):
    me = lax.axis_index("mem")
    z, c = me // 2, me % 2
    band = lax.axis_index("lat")
    lower = (band + 15) % 16
    loads = [
        pltpu.make_async_copy(eq_hbm, eq, sem.at[0]),
        pltpu.make_async_copy(inn_hbm, inn, sem.at[1]),
        pltpu.make_async_copy(index_hbm.at[band], rows_here, sem.at[2]),
        pltpu.make_async_copy(index_hbm.at[lower], rows_low, sem.at[3]),
    ]
    for load in loads:
        load.start()
    fill_starts(region_ref, band, starts)
    fill_starts(region_ref, lower, low_starts)
    start = starts[me]
    second = jnp.minimum(start + 1, BAND - 1)
    var_loads = [
        pltpu.make_async_copy(var_hbm.at[block], var_out.at[n], sem.at[4 + n])
        for n, block in enumerate((start, second))
    ]
    for load in var_loads:
        load.start()

    def block_cols(i, slot):
        first = starts[peer_of(i, z, c)]
        return pl.ds(pl.multiple_of(jnp.minimum(first + slot, BAND - 1) * BLOCK, BLOCK), BLOCK)

    inv_centre = 1.0 / coefficients(lo_ref[0], hi_ref[0])[0]
    loads[0].wait()
    top = lax.broadcasted_iota(jnp.int32, (12, BLOCK), 0) == 0

    def pack_pert(i, carry):
        lows = []
        for slot in range(2):
            values = eq[:, block_cols(i, slot)]
            total = jnp.sum(values, axis=0, keepdims=True) * (1.0 / ROOT)
            shift = (total - values[0:1]) * (1.0 / (ROOT - 1.0))
            mixed = jnp.where(top, total, (values - shift) * INV).astype(BF)
            send_p[i, slot] = mixed.reshape(3, 4, BLOCK)
            low = total - total.astype(BF).astype(F32)
            lows += [low[:, 0:256], low[:, 256:512]]
        send_low[i] = jnp.concatenate(lows, axis=0).astype(BF)
        return carry

    lax.fori_loop(0, 32, pack_pert, 0)
    for load in loads[2:]:
        load.wait()
    one = lambda on: jnp.where(on, 1.0, 0.0).astype(F32)
    pick[0] = one(rows_here[start, 0] == 1)
    pick[1] = one(rows_here[second, 0] == 1)
    pick[2] = one(rows_here[start, 1] == 1)
    pick[3] = one(rows_here[start, 2] == 1)
    pick[4] = one(rows_low[low_starts[me], 2] == 1)
    pick[5] = one((region_ref[band, me] > 1) & (mask_ref[band, start] == 1))
    loads[1].wait()

    def pack_rhs(i, carry):
        for slot in range(2):
            values = inn[:, block_cols(i, slot)]
            send_r[i, slot] = (values * inv_centre).astype(BF).reshape(3, 4, BLOCK)
        return carry

    lax.fori_loop(0, 32, pack_rhs, 0)
    for load in var_loads:
        load.wait()


def pack(equivalents, innovations, variance, index, regions, mask, low, high):
    chunk = (3, 4, BLOCK)
    return pl.pallas_call(
        pack_kernel,
        out_shape=(
            jax.ShapeDtypeStruct((32, 2) + chunk, BF),
            jax.ShapeDtypeStruct((32, 4, 256), BF),
            jax.ShapeDtypeStruct((32, 2) + chunk, BF),
            jax.ShapeDtypeStruct((2, 1, BLOCK), F32),
            jax.ShapeDtypeStruct((8,), F32),
        ),
        in_specs=[HB, HB, HB, HB, SM, SM, SM, SM],
        out_specs=(VM, VM, VM, VM, SM),
        scratch_shapes=[
            pltpu.VMEM((12, BAND * BLOCK), F32),
            pltpu.VMEM((12, BAND * BLOCK), F32),
            pltpu.SMEM((BAND, 3), jnp.int32),
            pltpu.SMEM((BAND, 3), jnp.int32),
            pltpu.SMEM((32,), jnp.int32),
            pltpu.SMEM((32,), jnp.int32),
            pltpu.SemaphoreType.DMA((6,)),
        ],
        name="pack",
    )(equivalents, innovations, variance, index, regions, mask, low, high)


def exchange_kernel(
    send_p, send_low, send_r, var_ref, taper_ref, pick, lo_ref, hi_ref,
    out_ref,
    got_p, got_low, got_r, send_w, pert, pert_up, pert_down, sym, flip, mat_a, mat_b,
    dir0_up, dir0_down, dir1, dir1_up, dir1_down, kept,
    sem_send, sem_own, sem_p, sem_low, sem_r, sem_w, sem_lat, sem_pert, sem_d0, sem_d1,
):
    me = lax.axis_index("mem")
    z, c = me // 2, me % 2
    band = lax.axis_index("lat")
    upper = (band + 1) % 16
    lower = (band + 15) % 16
    barrier = pltpu.get_barrier_semaphore()

    def greet(i, carry):
        pl.semaphore_signal(barrier, inc=1, device_id={"mem": peer_of(i, z, c)}, device_id_type=MESH)
        return carry

    lax.fori_loop(0, 31, greet, 0)
    for other in (upper, lower):
        pl.semaphore_signal(barrier, inc=1, device_id={"lat": other}, device_id_type=MESH)

    centre, rho1, sig1, rho2, sig2 = coefficients(lo_ref[0], hi_ref[0])
    for n in range(2):
        tile = taper_ref[n].astype(F32)
        turned = tile.T
        sym[n] = 0.5 * (tile + turned)
        flip[n] = turned.astype(BF)

    pl.semaphore_wait(barrier, 33)

    def remote(src, dst, recv, i):
        return pltpu.make_async_remote_copy(
            src_ref=src, dst_ref=dst, send_sem=sem_send, recv_sem=recv,
            device_id={"mem": peer_of(i, z, c)}, device_id_type=MESH,
        )

    def spread(send, got, sems):
        for i in (0, 1):
            remote(send.at[i], got.at[i], sems.at[0], i).start()

        def one(i, carry):
            j = mirror(i)
            remote(send.at[i], got.at[j], sems.at[j // 8], i).start()
            return carry

        lax.fori_loop(2, 30, one, 0)
        remote(send.at[30], got.at[30], sems.at[3], 30).start()

    def arrived(got, sems, g):
        size = 8 if g < 3 else 7
        view = got.at[pl.ds(8 * g, size)]
        pltpu.make_async_copy(view, view, sems.at[g]).wait()

    spread(send_p, got_p, sem_p)
    spread(send_low, got_low, sem_low)
    spread(send_r, got_r, sem_r)
    own = [
        pltpu.make_async_copy(sent.at[31], got.at[31], sem_own.at[n])
        for n, (sent, got) in enumerate(
            ((send_p, got_p), (send_low, got_low), (send_r, got_r), (send_w, out_ref))
        )
    ]
    for copy in own[:3]:
        copy.start()

    for g in range(GROUPS):
        arrived(got_p, sem_p, g)
        arrived(got_low, sem_low, g)
    own[0].wait()
    own[1].wait()
    lows = got_low[...].reshape(128, 256)
    row = lax.broadcasted_iota(jnp.int32, (M, M), 0)
    col = lax.broadcasted_iota(jnp.int32, (M, M), 1)
    spot = row % 12 == 0
    centring = jnp.where(row == col, 1.0, 0.0) - 1.0 / 32.0
    centring = jnp.where(spot & (col % 12 == 0), centring, 0.0).astype(BF)
    wide_row = lax.broadcasted_iota(jnp.int32, (M, 128), 0)
    wide_col = lax.broadcasted_iota(jnp.int32, (M, 128), 1)
    part_of = jnp.where(wide_row == 12 * (wide_col // 4), 1.0, 0.0) - 1.0 / 32.0
    is_mean = lax.broadcasted_iota(jnp.int32, (M, BLOCK), 0) % 12 == 0
    for slot in range(2):
        raw = got_p[:, slot].reshape(M, BLOCK)
        halves = []
        for half in range(2):
            use = (wide_row % 12 == 0) & (wide_col % 4 == 2 * slot + half)
            weight = jnp.where(use, part_of, 0.0).astype(BF)
            halves.append(jnp.dot(weight, lows, preferred_element_type=F32))
        centred = jnp.dot(centring, raw, preferred_element_type=F32)
        centred = (centred + jnp.concatenate(halves, axis=1)) * INV
        pert[slot] = jnp.where(is_mean, centred, raw.astype(F32)).astype(BF)

    def to_lat(src, dst, recv, other):
        return pltpu.make_async_remote_copy(
            src_ref=src, dst_ref=dst, send_sem=sem_lat, recv_sem=recv,
            device_id={"lat": other}, device_id_type=MESH,
        )

    def to_both(src, dst_down, dst_up, sem_down, sem_up):
        to_lat(src, dst_down, sem_down, upper).start()
        to_lat(src, dst_up, sem_up, lower).start()

    def landed(view, sem):
        pltpu.make_async_copy(view, view, sem).wait()

    to_both(pert.at[0], pert_down, pert_up, sem_pert.at[0], sem_pert.at[1])
    north_on = jnp.where(band < 15, 1.0, 0.0).astype(F32)
    south_on = jnp.where(band > 0, 1.0, 0.0).astype(F32)

    def build(dst, base, left, right, tiles, which, on):
        def chunk(r, carry):
            rows = pl.ds(pl.multiple_of(r * 128, 128), 128)
            prod = lax.dot_general(
                left[:, rows], right[...], (((0,), (0,)), ((), ())), preferred_element_type=F32
            )
            share = pick[which]
            tile = tiles[1, rows].astype(F32) * share + tiles[0, rows].astype(F32) * (1.0 - share)
            value = tile * prod
            if on is not None:
                value = value * on
            dst[pl.ds(pl.multiple_of(base + r * 128, 128), 128)] = value.astype(BF)
            return carry

        lax.fori_loop(0, 4, chunk, 0)

    here0, here1 = pert.at[0], pert.at[1]
    build(mat_a, 0, here0, here0, sym, 0, None)
    build(mat_a, 512, here1, here0, flip, 2, pick[5])
    build(mat_b, 0, here0, here1, taper_ref, 2, pick[5])
    build(mat_b, 512, here1, here1, sym, 1, None)
    landed(pert_up, sem_pert.at[1])
    landed(pert_down, sem_pert.at[0])
    build(mat_a, 1024, pert_up, here0, flip, 3, north_on)
    build(mat_a, 1536, pert_down, here0, taper_ref, 4, south_on)

    var = (var_ref[0], var_ref[1])
    keep_d = [rho1 + sig1 * (centre - v) for v in var]
    keep_y = [(1.0 + rho2 - sig2 * v) * sig1 + sig2 for v in var]

    def times(parts, mat):
        total = None
        for n, part in enumerate(parts):
            prod = jnp.dot(part, mat[pl.ds(512 * n, 512)], preferred_element_type=F32)
            total = prod if total is None else total + prod
        return total

    def stage_a(g):
        arrived(got_r, sem_r, g)
        if g == 3:
            own[2].wait()
        rows = pl.ds(8 * g, 8)
        to_both(
            got_r.at[rows, 0], dir0_down.at[rows], dir0_up.at[rows],
            sem_d0.at[g, 0], sem_d0.at[g, 1],
        )

    def stage_b(g):
        rows = pl.ds(8 * g, 8)
        landed(dir0_up.at[rows], sem_d0.at[g, 1])
        landed(dir0_down.at[rows], sem_d0.at[g, 0])
        mine = [got_r[rows, s].reshape(96, BLOCK) for s in range(2)]
        above = dir0_up[rows].reshape(96, BLOCK)
        below = dir0_down[rows].reshape(96, BLOCK)
        prods = (times((mine[0], mine[1], above, below), mat_a), times(mine, mat_b))
        for s in range(2):
            dir1[g, s] = (keep_d[s] * mine[s].astype(F32) - sig1 * prods[s]).astype(BF)
            kept[g, s] = keep_y[s] * prods[s]
        to_both(
            dir1.at[g, 0], dir1_down.at[g], dir1_up.at[g], sem_d1.at[g, 0], sem_d1.at[g, 1]
        )

    def stage_c(g):
        landed(dir1_up.at[g], sem_d1.at[g, 1])
        landed(dir1_down.at[g], sem_d1.at[g, 0])
        mine = [dir1[g, s] for s in range(2)]
        prods = (
            times((mine[0], mine[1], dir1_up[g], dir1_down[g]), mat_a), times(mine, mat_b)
        )
        for s in range(2):
            total = (kept[g, s] + sig2 * prods[s]).astype(BF)
            send_w[pl.ds(8 * g, 8), s] = total.reshape(8, 3, 4, BLOCK)
        for i in range(8 * g, 8 * g + 8):
            if i == 31:
                continue
            j = i if i < 2 or i == 30 else mirror(i)
            remote(send_w.at[i], out_ref.at[j], sem_w, i).start()

    stage_a(0)
    stage_a(1)
    stage_b(0)
    stage_a(2)
    stage_b(1)
    stage_c(0)
    stage_a(3)
    stage_b(2)
    stage_c(1)
    stage_b(3)
    stage_c(2)
    stage_c(3)
    own[3].start()
    own[3].wait()

    most = pl.ds(0, 31)
    landed(out_ref.at[most], sem_w)
    for sent in (send_p, send_low, send_r, send_w):
        pltpu.make_async_copy(sent.at[most], sent.at[most], sem_send).wait()
    for _ in range(2):
        pltpu.make_async_copy(pert.at[0], pert.at[0], sem_lat).wait()
        pltpu.make_async_copy(dir0_up, dir0_up, sem_lat).wait()
        pltpu.make_async_copy(dir1_up, dir1_up, sem_lat).wait()


def exchange(send_p, send_low, send_r, variance, tapers, pick, low, high):
    chunk = (3, 4, BLOCK)
    dma = pltpu.SemaphoreType.DMA
    return pl.pallas_call(
        exchange_kernel,
        out_shape=jax.ShapeDtypeStruct((32, 2) + chunk, BF),
        in_specs=[VM, VM, VM, VM, VM, SM, SM, SM],
        out_specs=VM,
        scratch_shapes=[
            pltpu.VMEM((32, 2) + chunk, BF),
            pltpu.VMEM((32, 4, 256), BF),
            pltpu.VMEM((32, 2) + chunk, BF),
            pltpu.VMEM((32, 2) + chunk, BF),
            pltpu.VMEM((2, M, BLOCK), BF),
            pltpu.VMEM((M, BLOCK), BF),
            pltpu.VMEM((M, BLOCK), BF),
            pltpu.VMEM((2, BLOCK, BLOCK), F32),
            pltpu.VMEM((2, BLOCK, BLOCK), BF),
            pltpu.VMEM((4 * BLOCK, BLOCK), BF),
            pltpu.VMEM((2 * BLOCK, BLOCK), BF),
            pltpu.VMEM((32,) + chunk, BF),
            pltpu.VMEM((32,) + chunk, BF),
            pltpu.VMEM((GROUPS, 2, 96, BLOCK), BF),
            pltpu.VMEM((GROUPS, 96, BLOCK), BF),
            pltpu.VMEM((GROUPS, 96, BLOCK), BF),
            pltpu.VMEM((GROUPS, 2, 96, BLOCK), F32),
            dma,
            dma((4,)),
            dma((GROUPS,)),
            dma((GROUPS,)),
            dma((GROUPS,)),
            dma,
            dma,
            dma((2,)),
            dma((GROUPS, 2)),
            dma((GROUPS, 2)),
        ],
        compiler_params=pltpu.CompilerParams(
            collective_id=0, has_side_effects=True, vmem_limit_bytes=48 << 20
        ),
        name="exchange",
    )(send_p, send_low, send_r, variance, tapers, pick, low, high)


STEPS = 6
PER_STEP = BAND // STEPS


def finish_kernel(inn_ref, var_ref, got_ref, region_ref, lo_ref, hi_ref, out_ref, where):
    me = lax.axis_index("mem")
    z, c = me // 2, me % 2
    band = lax.axis_index("lat")
    step = pl.program_id(0)

    @pl.when(step == 0)
    def _():
        def one(m, total):
            dz = (m // 2 - z + 16) % 16
            t = jnp.where(dz < 8, 15 - 2 * dz, 2 * dz - 16)
            place = 2 * t + 1 - (m + c) % 2
            where[jnp.minimum(total + 1, BAND - 1)] = 2 * place + 1
            where[total] = 2 * place
            return total + region_ref[band, m]

        lax.fori_loop(0, 32, one, jnp.int32(0))

    centre, rho1, sig1, rho2, sig2 = coefficients(lo_ref[0], hi_ref[0])
    for n in range(PER_STEP):
        cols = pl.ds(n * BLOCK, BLOCK)
        var = var_ref[n]
        keep = rho1 + sig1 * (centre - var)
        factor = 1.0 + (1.0 + rho2 - sig2 * var) * keep + sig2 * (centre - var)
        entry = where[step * PER_STEP + n]
        local = (factor / centre) * inn_ref[:, cols]
        out_ref[:, cols] = local - got_ref[entry // 2, entry % 2].reshape(12, BLOCK).astype(F32)


def finish(innovations, variance, got, regions, low, high):
    width = PER_STEP * BLOCK
    return pl.pallas_call(
        finish_kernel,
        grid=(STEPS,),
        out_shape=jax.ShapeDtypeStruct((12, BAND * BLOCK), F32),
        in_specs=[
            pl.BlockSpec((12, width), lambda i: (0, i)),
            pl.BlockSpec((PER_STEP, 1, BLOCK), lambda i: (i, 0, 0)),
            VM, SM, SM, SM,
        ],
        out_specs=pl.BlockSpec((12, width), lambda i: (0, i)),
        scratch_shapes=[pltpu.SMEM((BAND,), jnp.int32)],
        name="finish",
    )(innovations, variance, got, regions, low, high)


def on_device(
    equivalents, innovations, obs_var, taper_tiles, region_blocks, pair_mask, taper_index,
    eig_low, eig_high,
):
    variance = obs_var.reshape(BAND, 1, BLOCK)
    send_p, send_low, send_r, own_var, pick = pack(
        equivalents, innovations, variance, taper_index, region_blocks, pair_mask, eig_low,
        eig_high,
    )
    got = exchange(send_p, send_low, send_r, own_var, taper_tiles, pick, eig_low, eig_high)
    return finish(innovations, variance, got, region_blocks, eig_low, eig_high)


def solution(mesh):
    return jax.shard_map(
        on_device,
        mesh=mesh,
        in_specs=(P("mem", "lat"), P("mem", "lat"), P("lat"), P(), P(), P(), P(), P(), P()),
        out_specs=P("mem", "lat"),
        check_vma=False,
    )
```

```python
import jax
import jax.numpy as jnp
from jax import lax
from jax.experimental import pallas as pl
from jax.experimental.pallas import tpu as pltpu
from jax.sharding import PartitionSpec as P

M = 384
BLOCK = 512
BAND = 48
GROUPS = 4
LIMIT = 60 * 1024 * 1024
BF = jnp.bfloat16
F32 = jnp.float32
MESH = pl.DeviceIdType.MESH
VM = pl.BlockSpec(memory_space=pltpu.VMEM)
HB = pl.BlockSpec(memory_space=pl.ANY)
SM = pl.BlockSpec(memory_space=pltpu.SMEM)
INV = (M - 1) ** -0.5


def coefficients(lo, hi):
    low = jnp.full((1, BLOCK), lo, F32)
    high = jnp.full((1, BLOCK), hi, F32)
    centre = 0.5 * (high + low)
    half = 0.5 * (high - low)
    scale = centre / half
    q0 = 1.0 / scale
    q1 = 1.0 / (2.0 * scale - q0)
    q2 = 1.0 / (2.0 * scale - q1)
    return centre, q1 * q0, 2.0 * q1 / half, q2 * q1, 2.0 * q2 / half


def peer_of(i, z, c):
    t = i // 2
    odd = t % 2
    dz = (8 - (t + 1) // 2) * (2 * odd - 1)
    return (z + dz + 16) % 16 * 2 + (c + 1 - i % 2) % 2


def mirror(i):
    t = i // 2
    return i + 4 * (t % 2) - 2


ROOT = 12.0**0.5


CUTS = 6


def pack_kernel(
    eq_hbm, inn_hbm, var_hbm, index_ref, region_ref, mask_ref, lo_ref, hi_ref,
    out_p, out_low, out_r, var_out, pick, where,
    eq, inn, send_p, send_low, send_r, starts, low_starts, sem_eq, sem_inn, sem_var, sem_out,
):
    me = lax.axis_index("mem")
    z, c = me // 2, me % 2
    band = lax.axis_index("lat")
    lower = (band + 15) % 16
    loads = []
    for source, target, sems in ((eq_hbm, eq, sem_eq), (inn_hbm, inn, sem_inn)):
        for n in range(CUTS):
            cols = pl.ds(n * (BAND * BLOCK // CUTS), BAND * BLOCK // CUTS)
            load = pltpu.make_async_copy(source.at[:, cols], target.at[:, cols], sems.at[n])
            load.start()
            loads.append(load)

    def scan(m, totals):
        total, low_total = totals
        starts[m] = total
        low_starts[m] = low_total
        dz = (m // 2 - z + 16) % 16
        t = jnp.where(dz < 8, 15 - 2 * dz, 2 * dz - 16)
        place = 2 * t + 1 - (m + c) % 2
        where[jnp.minimum(total + 1, BAND - 1)] = 2 * place + 1
        where[total] = 2 * place
        return total + region_ref[band, m], low_total + region_ref[lower, m]

    lax.fori_loop(0, 32, scan, (jnp.int32(0), jnp.int32(0)))
    start = starts[me]
    second = jnp.minimum(start + 1, BAND - 1)
    var_loads = [
        pltpu.make_async_copy(var_hbm.at[block], var_out.at[n], sem_var.at[n])
        for n, block in enumerate((start, second))
    ]
    for load in var_loads:
        load.start()

    def one(on):
        return jnp.where(on, 1.0, 0.0).astype(F32)

    pick[0] = one(index_ref[0, band, start] == 1)
    pick[1] = one(index_ref[0, band, second] == 1)
    pick[2] = one(index_ref[1, band, start] == 1)
    pick[3] = one(index_ref[2, band, start] == 1)
    pick[4] = one(index_ref[2, lower, low_starts[me]] == 1)
    pick[5] = one((region_ref[band, me] > 1) & (mask_ref[band, start] == 1))
    pick[6] = one(band < 15)
    pick[7] = one(band > 0)

    def block_cols(i, slot):
        first = starts[peer_of(i, z, c)]
        return pl.ds(pl.multiple_of(jnp.minimum(first + slot, BAND - 1) * BLOCK, BLOCK), BLOCK)

    inv_centre = 1.0 / coefficients(lo_ref[0], hi_ref[0])[0]
    top = lax.broadcasted_iota(jnp.int32, (12, BLOCK), 0) == 0
    for load in loads[:CUTS]:
        load.wait()

    def pack_pert(i, carry):
        lows = []
        for slot in range(2):
            values = eq[:, block_cols(i, slot)]
            total = jnp.sum(values, axis=0, keepdims=True) * (1.0 / ROOT)
            shift = (total - values[0:1]) * (1.0 / (ROOT - 1.0))
            mixed = jnp.where(top, total, (values - shift) * INV).astype(BF)
            send_p[i, slot] = mixed.reshape(3, 4, BLOCK)
            low = total - total.astype(BF).astype(F32)
            lows += [low[:, 0:256], low[:, 256:512]]
        send_low[i] = jnp.concatenate(lows, axis=0).astype(BF)
        return carry

    lax.fori_loop(0, 32, pack_pert, 0, unroll=2)
    stores = [
        pltpu.make_async_copy(send_p, out_p, sem_out.at[0]),
        pltpu.make_async_copy(send_low, out_low, sem_out.at[1]),
        pltpu.make_async_copy(send_r, out_r, sem_out.at[2]),
    ]
    stores[0].start()
    stores[1].start()
    for load in loads[CUTS:]:
        load.wait()

    def pack_rhs(i, carry):
        for slot in range(2):
            values = inn[:, block_cols(i, slot)]
            send_r[i, slot] = (values * inv_centre).astype(BF).reshape(3, 4, BLOCK)
        return carry

    lax.fori_loop(0, 32, pack_rhs, 0, unroll=4)
    stores[2].start()
    for copy in var_loads + stores:
        copy.wait()


def pack(equivalents, innovations, variance, index, regions, mask, low, high):
    chunks = (32, 2, 3, 4, BLOCK)
    lows = (32, 4, 256)
    dma = pltpu.SemaphoreType.DMA
    return pl.pallas_call(
        pack_kernel,
        out_shape=(
            jax.ShapeDtypeStruct(chunks, BF),
            jax.ShapeDtypeStruct(lows, BF),
            jax.ShapeDtypeStruct(chunks, BF),
            jax.ShapeDtypeStruct((2, 1, BLOCK), F32),
            jax.ShapeDtypeStruct((8,), F32),
            jax.ShapeDtypeStruct((BAND,), jnp.int32),
        ),
        in_specs=[HB, HB, HB, SM, SM, SM, SM, SM],
        out_specs=(HB, HB, HB, VM, SM, SM),
        scratch_shapes=[
            pltpu.VMEM((12, BAND * BLOCK), F32),
            pltpu.VMEM((12, BAND * BLOCK), F32),
            pltpu.VMEM(chunks, BF),
            pltpu.VMEM(lows, BF),
            pltpu.VMEM(chunks, BF),
            pltpu.SMEM((32,), jnp.int32),
            pltpu.SMEM((32,), jnp.int32),
            dma((CUTS,)),
            dma((CUTS,)),
            dma((2,)),
            dma((3,)),
        ],
        compiler_params=pltpu.CompilerParams(vmem_limit_bytes=LIMIT),
        name="pack",
    )(equivalents, innovations, variance, index, regions, mask, low, high)


def exchange_kernel(
    send_p, send_low, send_r, var_hbm, taper_hbm, pick, lo_ref, hi_ref,
    out_ref,
    var_ref, taper_ref,
    got_p, got_low, got_r, send_w, pert, pert_up, pert_down, sym, flip, mat_a, mat_b,
    dir0_up, dir0_down, dir1, dir1_up, dir1_down, kept,
    sem_send, sem_own, sem_p, sem_low, sem_r, sem_w, sem_lat, sem_pert, sem_d0, sem_d1,
):
    me = lax.axis_index("mem")
    z, c = me // 2, me % 2
    band = lax.axis_index("lat")
    upper = (band + 1) % 16
    lower = (band + 15) % 16
    fetches = [
        pltpu.make_async_copy(taper_hbm, taper_ref, sem_own.at[4]),
        pltpu.make_async_copy(var_hbm, var_ref, sem_own.at[5]),
    ]
    for fetch in fetches:
        fetch.start()
    barrier = pltpu.get_barrier_semaphore()

    def greet(i, carry):
        pl.semaphore_signal(barrier, inc=1, device_id={"mem": peer_of(i, z, c)}, device_id_type=MESH)
        return carry

    lax.fori_loop(0, 31, greet, 0)
    for other in (upper, lower):
        pl.semaphore_signal(barrier, inc=1, device_id={"lat": other}, device_id_type=MESH)

    centre, rho1, sig1, rho2, sig2 = coefficients(lo_ref[0], hi_ref[0])
    for fetch in fetches:
        fetch.wait()
    for n in range(2):
        tile = taper_ref[n].astype(F32)
        turned = tile.T
        sym[n] = 0.5 * (tile + turned)
        flip[n] = turned.astype(BF)

    pl.semaphore_wait(barrier, 33)

    def remote(src, dst, recv, i):
        return pltpu.make_async_remote_copy(
            src_ref=src, dst_ref=dst, send_sem=sem_send, recv_sem=recv,
            device_id={"mem": peer_of(i, z, c)}, device_id_type=MESH,
        )

    def spread(send, got, sems):
        for i in (0, 1):
            remote(send.at[i], got.at[i], sems.at[0], i).start()

        def one(i, carry):
            j = mirror(i)
            remote(send.at[i], got.at[j], sems.at[j // 8], i).start()
            return carry

        lax.fori_loop(2, 30, one, 0)
        remote(send.at[30], got.at[30], sems.at[3], 30).start()

    def arrived(got, sems, g):
        size = 8 if g < 3 else 7
        view = got.at[pl.ds(8 * g, size)]
        pltpu.make_async_copy(view, view, sems.at[g]).wait()

    spread(send_p, got_p, sem_p)
    spread(send_low, got_low, sem_low)
    spread(send_r, got_r, sem_r)
    own = [
        pltpu.make_async_copy(sent.at[31], got.at[31], sem_own.at[n])
        for n, (sent, got) in enumerate(
            ((send_p, got_p), (send_low, got_low), (send_r, got_r), (send_w, out_ref))
        )
    ]
    for copy in own[:3]:
        copy.start()

    for g in range(GROUPS):
        arrived(got_p, sem_p, g)
        arrived(got_low, sem_low, g)
    own[0].wait()
    own[1].wait()
    lows = got_low[...].reshape(128, 256)
    row = lax.broadcasted_iota(jnp.int32, (M, M), 0)
    col = lax.broadcasted_iota(jnp.int32, (M, M), 1)
    spot = row % 12 == 0
    centring = jnp.where(row == col, 1.0, 0.0) - 1.0 / 32.0
    centring = jnp.where(spot & (col % 12 == 0), centring, 0.0).astype(BF)
    wide_row = lax.broadcasted_iota(jnp.int32, (M, 128), 0)
    wide_col = lax.broadcasted_iota(jnp.int32, (M, 128), 1)
    part_of = jnp.where(wide_row == 12 * (wide_col // 4), 1.0, 0.0) - 1.0 / 32.0
    is_mean = lax.broadcasted_iota(jnp.int32, (M, BLOCK), 0) % 12 == 0
    for slot in range(2):
        raw = got_p[:, slot].reshape(M, BLOCK)
        halves = []
        for half in range(2):
            use = (wide_row % 12 == 0) & (wide_col % 4 == 2 * slot + half)
            weight = jnp.where(use, part_of, 0.0).astype(BF)
            halves.append(jnp.dot(weight, lows, preferred_element_type=F32))
        centred = jnp.dot(centring, raw, preferred_element_type=F32)
        centred = (centred + jnp.concatenate(halves, axis=1)) * INV
        pert[slot] = jnp.where(is_mean, centred, raw.astype(F32)).astype(BF)

    def to_lat(src, dst, recv, other):
        return pltpu.make_async_remote_copy(
            src_ref=src, dst_ref=dst, send_sem=sem_lat, recv_sem=recv,
            device_id={"lat": other}, device_id_type=MESH,
        )

    def to_both(src, dst_down, dst_up, sem_down, sem_up):
        to_lat(src, dst_down, sem_down, upper).start()
        to_lat(src, dst_up, sem_up, lower).start()

    def landed(view, sem):
        pltpu.make_async_copy(view, view, sem).wait()

    to_both(pert.at[0], pert_down, pert_up, sem_pert.at[0], sem_pert.at[1])
    north_on = pick[6]
    south_on = pick[7]

    def build(dst, base, left, right, tiles, which, on):
        def chunk(r, carry):
            rows = pl.ds(pl.multiple_of(r * 128, 128), 128)
            prod = lax.dot_general(
                left[:, rows], right[...], (((0,), (0,)), ((), ())), preferred_element_type=F32
            )
            share = pick[which]
            tile = tiles[1, rows].astype(F32) * share + tiles[0, rows].astype(F32) * (1.0 - share)
            value = tile * prod
            if on is not None:
                value = value * on
            dst[pl.ds(pl.multiple_of(base + r * 128, 128), 128)] = value.astype(BF)
            return carry

        lax.fori_loop(0, 4, chunk, 0)

    here0, here1 = pert.at[0], pert.at[1]
    build(mat_a, 0, here0, here0, sym, 0, None)
    build(mat_a, 512, here1, here0, flip, 2, pick[5])
    build(mat_b, 0, here0, here1, taper_ref, 2, pick[5])
    build(mat_b, 512, here1, here1, sym, 1, None)
    landed(pert_up, sem_pert.at[1])
    landed(pert_down, sem_pert.at[0])
    build(mat_a, 1024, pert_up, here0, flip, 3, north_on)
    build(mat_a, 1536, pert_down, here0, taper_ref, 4, south_on)

    var = (var_ref[0], var_ref[1])
    keep_d = [rho1 + sig1 * (centre - v) for v in var]
    keep_y = [(1.0 + rho2 - sig2 * v) * sig1 + sig2 for v in var]

    def times(parts, mat):
        total = None
        for n, part in enumerate(parts):
            prod = jnp.dot(part, mat[pl.ds(512 * n, 512)], preferred_element_type=F32)
            total = prod if total is None else total + prod
        return total

    def stage_a(g):
        arrived(got_r, sem_r, g)
        if g == 3:
            own[2].wait()
        rows = pl.ds(8 * g, 8)
        to_both(
            got_r.at[rows, 0], dir0_down.at[rows], dir0_up.at[rows],
            sem_d0.at[g, 0], sem_d0.at[g, 1],
        )

    def stage_b(g):
        rows = pl.ds(8 * g, 8)
        landed(dir0_up.at[rows], sem_d0.at[g, 1])
        landed(dir0_down.at[rows], sem_d0.at[g, 0])
        mine = [got_r[rows, s].reshape(96, BLOCK) for s in range(2)]
        above = dir0_up[rows].reshape(96, BLOCK)
        below = dir0_down[rows].reshape(96, BLOCK)
        prods = (times((mine[0], mine[1], above, below), mat_a), times(mine, mat_b))
        for s in range(2):
            dir1[g, s] = (keep_d[s] * mine[s].astype(F32) - sig1 * prods[s]).astype(BF)
            kept[g, s] = keep_y[s] * prods[s]
        to_both(
            dir1.at[g, 0], dir1_down.at[g], dir1_up.at[g], sem_d1.at[g, 0], sem_d1.at[g, 1]
        )

    def stage_c(g):
        landed(dir1_up.at[g], sem_d1.at[g, 1])
        landed(dir1_down.at[g], sem_d1.at[g, 0])
        mine = [dir1[g, s] for s in range(2)]
        prods = (
            times((mine[0], mine[1], dir1_up[g], dir1_down[g]), mat_a), times(mine, mat_b)
        )
        for s in range(2):
            total = (kept[g, s] + sig2 * prods[s]).astype(BF)
            send_w[pl.ds(8 * g, 8), s] = total.reshape(8, 3, 4, BLOCK)
        for i in range(8 * g, 8 * g + 8):
            if i == 31:
                continue
            j = i if i < 2 or i == 30 else mirror(i)
            remote(send_w.at[i], out_ref.at[j], sem_w, i).start()

    stage_a(0)
    stage_a(1)
    stage_b(0)
    stage_a(2)
    stage_b(1)
    stage_c(0)
    stage_a(3)
    stage_b(2)
    stage_c(1)
    stage_b(3)
    stage_c(2)
    stage_c(3)
    own[3].start()
    own[3].wait()

    most = pl.ds(0, 31)
    landed(out_ref.at[most], sem_w)
    for sent in (send_p, send_low, send_r, send_w):
        pltpu.make_async_copy(sent.at[most], sent.at[most], sem_send).wait()
    for _ in range(2):
        pltpu.make_async_copy(pert.at[0], pert.at[0], sem_lat).wait()
        pltpu.make_async_copy(dir0_up, dir0_up, sem_lat).wait()
        pltpu.make_async_copy(dir1_up, dir1_up, sem_lat).wait()


def exchange(send_p, send_low, send_r, variance, tapers, pick, low, high):
    chunk = (3, 4, BLOCK)
    dma = pltpu.SemaphoreType.DMA
    return pl.pallas_call(
        exchange_kernel,
        out_shape=jax.ShapeDtypeStruct((32, 2) + chunk, BF),
        in_specs=[HB, HB, HB, HB, HB, SM, SM, SM],
        out_specs=HB,
        scratch_shapes=[
            pltpu.VMEM((2, 1, BLOCK), F32),
            pltpu.VMEM((2, BLOCK, BLOCK), BF),
            pltpu.VMEM((32, 2) + chunk, BF),
            pltpu.VMEM((32, 4, 256), BF),
            pltpu.VMEM((32, 2) + chunk, BF),
            pltpu.VMEM((32, 2) + chunk, BF),
            pltpu.VMEM((2, M, BLOCK), BF),
            pltpu.VMEM((M, BLOCK), BF),
            pltpu.VMEM((M, BLOCK), BF),
            pltpu.VMEM((2, BLOCK, BLOCK), F32),
            pltpu.VMEM((2, BLOCK, BLOCK), BF),
            pltpu.VMEM((4 * BLOCK, BLOCK), BF),
            pltpu.VMEM((2 * BLOCK, BLOCK), BF),
            pltpu.VMEM((32,) + chunk, BF),
            pltpu.VMEM((32,) + chunk, BF),
            pltpu.VMEM((GROUPS, 2, 96, BLOCK), BF),
            pltpu.VMEM((GROUPS, 96, BLOCK), BF),
            pltpu.VMEM((GROUPS, 96, BLOCK), BF),
            pltpu.VMEM((GROUPS, 2, 96, BLOCK), F32),
            dma,
            dma((6,)),
            dma((GROUPS,)),
            dma((GROUPS,)),
            dma((GROUPS,)),
            dma,
            dma,
            dma((2,)),
            dma((GROUPS, 2)),
            dma((GROUPS, 2)),
        ],
        compiler_params=pltpu.CompilerParams(
            collective_id=0, has_side_effects=True, vmem_limit_bytes=LIMIT
        ),
        name="exchange",
    )(send_p, send_low, send_r, variance, tapers, pick, low, high)


STEPS = 4
PER_STEP = BAND // STEPS


def finish_kernel(inn_ref, var_ref, got_ref, where, lo_ref, hi_ref, out_ref):
    step = pl.program_id(0)
    centre, rho1, sig1, rho2, sig2 = coefficients(lo_ref[0], hi_ref[0])
    inv_centre = 1.0 / centre
    for n in range(PER_STEP):
        cols = pl.ds(n * BLOCK, BLOCK)
        var = var_ref[n]
        keep = rho1 + sig1 * (centre - var)
        factor = 1.0 + (1.0 + rho2 - sig2 * var) * keep + sig2 * (centre - var)
        entry = where[step * PER_STEP + n]
        local = (factor * inv_centre) * inn_ref[:, cols]
        out_ref[:, cols] = local - got_ref[entry // 2, entry % 2].reshape(12, BLOCK).astype(F32)


def finish(innovations, variance, got, where, low, high):
    width = PER_STEP * BLOCK
    return pl.pallas_call(
        finish_kernel,
        grid=(STEPS,),
        out_shape=jax.ShapeDtypeStruct((12, BAND * BLOCK), F32),
        in_specs=[
            pl.BlockSpec((12, width), lambda i: (0, i)),
            pl.BlockSpec((PER_STEP, 1, BLOCK), lambda i: (i, 0, 0)),
            VM, SM, SM, SM,
        ],
        out_specs=pl.BlockSpec((12, width), lambda i: (0, i)),
        name="finish",
    )(innovations, variance, got, where, low, high)


def on_device(
    equivalents, innovations, obs_var, taper_tiles, region_blocks, pair_mask, taper_index,
    eig_low, eig_high,
):
    variance = obs_var.reshape(BAND, 1, BLOCK)
    send_p, send_low, send_r, own_var, pick, where = pack(
        equivalents, innovations, variance, jnp.transpose(taper_index, (2, 0, 1)), region_blocks, pair_mask, eig_low,
        eig_high,
    )
    got = exchange(send_p, send_low, send_r, own_var, taper_tiles, pick, eig_low, eig_high)
    return finish(innovations, variance, got, where, eig_low, eig_high)


def solution(mesh):
    return jax.shard_map(
        on_device,
        mesh=mesh,
        in_specs=(P("mem", "lat"), P("mem", "lat"), P("lat"), P(), P(), P(), P(), P(), P()),
        out_specs=P("mem", "lat"),
        check_vma=False,
    )
```

```python
import jax
import jax.numpy as jnp
from jax import lax
from jax.experimental import pallas as pl
from jax.experimental.pallas import tpu as pltpu
from jax.sharding import PartitionSpec as P

M = 384
BLOCK = 512
BAND = 48
GROUPS = 4
LIMIT = 60 * 1024 * 1024
BF = jnp.bfloat16
F32 = jnp.float32
MESH = pl.DeviceIdType.MESH
VM = pl.BlockSpec(memory_space=pltpu.VMEM)
HB = pl.BlockSpec(memory_space=pl.ANY)
SM = pl.BlockSpec(memory_space=pltpu.SMEM)
INV = (M - 1) ** -0.5


def coefficients(lo, hi):
    low = jnp.full((1, BLOCK), lo, F32)
    high = jnp.full((1, BLOCK), hi, F32)
    centre = 0.5 * (high + low)
    half = 0.5 * (high - low)
    scale = centre / half
    q0 = 1.0 / scale
    q1 = 1.0 / (2.0 * scale - q0)
    q2 = 1.0 / (2.0 * scale - q1)
    return centre, q1 * q0, 2.0 * q1 / half, q2 * q1, 2.0 * q2 / half


def peer_of(i, z, c):
    t = i // 2
    odd = t % 2
    dz = (8 - (t + 1) // 2) * (2 * odd - 1)
    return (z + dz + 16) % 16 * 2 + (c + 1 - i % 2) % 2


def mirror(i):
    t = i // 2
    return i + 4 * (t % 2) - 2


ROOT = 12.0**0.5


def tables_kernel(index_ref, region_ref, mask_ref, blocks, pick, where, starts, low_starts):
    me = lax.axis_index("mem")
    z, c = me // 2, me % 2
    band = lax.axis_index("lat")
    lower = (band + 15) % 16

    def scan(m, totals):
        total, low_total = totals
        starts[m] = total
        low_starts[m] = low_total
        dz = (m // 2 - z + 16) % 16
        t = jnp.where(dz < 8, 15 - 2 * dz, 2 * dz - 16)
        place = 2 * (2 * t + 1 - (m + c) % 2)
        follow = jnp.minimum(total + 1, BAND - 1)
        where[follow] = place + 1
        where[total] = place
        blocks[place] = total
        blocks[place + 1] = follow
        return total + region_ref[band, m], low_total + region_ref[lower, m]

    lax.fori_loop(0, 32, scan, (jnp.int32(0), jnp.int32(0)), unroll=4)
    start = starts[me]
    second = jnp.minimum(start + 1, BAND - 1)

    def one(on):
        return jnp.where(on, 1.0, 0.0).astype(F32)

    pick[0] = one(index_ref[0, band, start] == 1)
    pick[1] = one(index_ref[0, band, second] == 1)
    pick[2] = one(index_ref[1, band, start] == 1)
    pick[3] = one(index_ref[2, band, start] == 1)
    pick[4] = one(index_ref[2, lower, low_starts[me]] == 1)
    pick[5] = one((region_ref[band, me] > 1) & (mask_ref[band, start] == 1))
    pick[6] = one(band < 15)
    pick[7] = one(band > 0)


def tables(index, regions, mask):
    return pl.pallas_call(
        tables_kernel,
        out_shape=(
            jax.ShapeDtypeStruct((64,), jnp.int32),
            jax.ShapeDtypeStruct((8,), F32),
            jax.ShapeDtypeStruct((BAND,), jnp.int32),
        ),
        in_specs=[SM, SM, SM],
        out_specs=(SM, SM, SM),
        scratch_shapes=[pltpu.SMEM((32,), jnp.int32), pltpu.SMEM((32,), jnp.int32)],
        name="tables",
    )(index, regions, mask)


def exchange_kernel(
    eq_hbm, inn_hbm, var_hbm, taper_hbm, blocks, pick, lo_ref, hi_ref,
    out_ref, base_hbm,
    base_ref,
    eq, inn, var_ref, taper_ref, send_p, send_low, send_r,
    got_p, got_low, got_r, send_w, pert, pert_up, pert_down, sym, flip, mat_a, mat_b,
    dir0_up, dir0_down, dir1, dir1_up, dir1_down, kept,
    sem_send, sem_own, sem_in, sem_p, sem_low, sem_r, sem_w, sem_lat, sem_pert, sem_d0, sem_d1,
):
    me = lax.axis_index("mem")
    z, c = me // 2, me % 2
    band = lax.axis_index("lat")
    upper = (band + 1) % 16
    lower = (band + 15) % 16

    def column(k):
        return pl.ds(pl.multiple_of(k * BLOCK, BLOCK), BLOCK)

    def fetch_block(source, target, n, k):
        return pltpu.make_async_copy(source.at[:, column(k)], target.at[k], sem_in.at[n, k])

    def start_fetch(source, target, n):
        def one(k, carry):
            fetch_block(source, target, n, k).start()
            return carry

        lax.fori_loop(0, BAND, one, 0)

    def end_fetch(source, target, n):
        def one(k, carry):
            fetch_block(source, target, n, k).wait()
            return carry

        lax.fori_loop(0, BAND, one, 0)

    barrier = pltpu.get_barrier_semaphore()

    def greet(i, carry):
        pl.semaphore_signal(barrier, inc=1, device_id={"mem": peer_of(i, z, c)}, device_id_type=MESH)
        return carry

    lax.fori_loop(0, 31, greet, 0)
    for other in (upper, lower):
        pl.semaphore_signal(barrier, inc=1, device_id={"lat": other}, device_id_type=MESH)

    centre, rho1, sig1, rho2, sig2 = coefficients(lo_ref[0], hi_ref[0])
    start_fetch(eq_hbm, eq, 0)
    start_fetch(inn_hbm, inn, 1)
    fetches = [
        pltpu.make_async_copy(taper_hbm, taper_ref, sem_own.at[4]),
        pltpu.make_async_copy(var_hbm, var_ref, sem_own.at[5]),
    ]
    for fetch in fetches:
        fetch.start()
    top = lax.broadcasted_iota(jnp.int32, (12, BLOCK), 0) == 0
    end_fetch(eq_hbm, eq, 0)

    def pack_pert(i, carry):
        lows = []
        for slot in range(2):
            values = eq[blocks[2 * i + slot]]
            total = jnp.sum(values, axis=0, keepdims=True) * (1.0 / ROOT)
            shift = (total - values[0:1]) * (1.0 / (ROOT - 1.0))
            mixed = jnp.where(top, total, (values - shift) * INV).astype(BF)
            send_p[i, slot] = mixed.reshape(3, 4, BLOCK)
            low = total - total.astype(BF).astype(F32)
            lows += [low[:, 0:256], low[:, 256:512]]
        send_low[i] = jnp.concatenate(lows, axis=0).astype(BF)
        return carry

    lax.fori_loop(0, 32, pack_pert, 0, unroll=2)
    pl.semaphore_wait(barrier, 33)

    def remote(src, dst, recv, i):
        return pltpu.make_async_remote_copy(
            src_ref=src, dst_ref=dst, send_sem=sem_send, recv_sem=recv,
            device_id={"mem": peer_of(i, z, c)}, device_id_type=MESH,
        )

    def spread(send, got, sems):
        for i in (0, 1):
            remote(send.at[i], got.at[i], sems.at[0], i).start()

        def one(i, carry):
            j = mirror(i)
            remote(send.at[i], got.at[j], sems.at[j // 8], i).start()
            return carry

        lax.fori_loop(2, 30, one, 0)
        remote(send.at[30], got.at[30], sems.at[3], 30).start()

    def arrived(got, sems, g):
        size = 8 if g < 3 else 7
        view = got.at[pl.ds(8 * g, size)]
        pltpu.make_async_copy(view, view, sems.at[g]).wait()

    spread(send_p, got_p, sem_p)
    spread(send_low, got_low, sem_low)
    inv_centre = 1.0 / centre
    end_fetch(inn_hbm, inn, 1)

    def pack_rhs(i, carry):
        for slot in range(2):
            values = inn[blocks[2 * i + slot]]
            send_r[i, slot] = (values * inv_centre).astype(BF).reshape(3, 4, BLOCK)
        return carry

    lax.fori_loop(0, 32, pack_rhs, 0, unroll=2)
    spread(send_r, got_r, sem_r)
    own = [
        pltpu.make_async_copy(sent.at[31], got.at[31], sem_own.at[n])
        for n, (sent, got) in enumerate(
            ((send_p, got_p), (send_low, got_low), (send_r, got_r), (send_w, out_ref))
        )
    ]
    for copy in own[:3]:
        copy.start()
    for fetch in fetches:
        fetch.wait()
    for n in range(2):
        tile = taper_ref[n].astype(F32)
        turned = tile.T
        sym[n] = 0.5 * (tile + turned)
        flip[n] = turned.astype(BF)


    def local_part(k, carry):
        var = var_ref[k]
        keep = rho1 + sig1 * (centre - var)
        factor = 1.0 + (1.0 + rho2 - sig2 * var) * keep + sig2 * (centre - var)
        base_ref[k] = (factor * inv_centre) * inn[k]
        return carry

    lax.fori_loop(0, BAND, local_part, 0)
    keep_base = pltpu.make_async_copy(base_ref, base_hbm, sem_own.at[6])
    keep_base.start()

    for g in range(GROUPS):
        arrived(got_p, sem_p, g)
        arrived(got_low, sem_low, g)
    own[0].wait()
    own[1].wait()
    lows = got_low[...].reshape(128, 256)
    row = lax.broadcasted_iota(jnp.int32, (M, M), 0)
    col = lax.broadcasted_iota(jnp.int32, (M, M), 1)
    spot = row % 12 == 0
    centring = jnp.where(row == col, 1.0, 0.0) - 1.0 / 32.0
    centring = jnp.where(spot & (col % 12 == 0), centring, 0.0).astype(BF)
    wide_row = lax.broadcasted_iota(jnp.int32, (M, 128), 0)
    wide_col = lax.broadcasted_iota(jnp.int32, (M, 128), 1)
    part_of = jnp.where(wide_row == 12 * (wide_col // 4), 1.0, 0.0) - 1.0 / 32.0
    is_mean = lax.broadcasted_iota(jnp.int32, (M, BLOCK), 0) % 12 == 0
    for slot in range(2):
        raw = got_p[:, slot].reshape(M, BLOCK)
        halves = []
        for half in range(2):
            use = (wide_row % 12 == 0) & (wide_col % 4 == 2 * slot + half)
            weight = jnp.where(use, part_of, 0.0).astype(BF)
            halves.append(jnp.dot(weight, lows, preferred_element_type=F32))
        centred = jnp.dot(centring, raw, preferred_element_type=F32)
        centred = (centred + jnp.concatenate(halves, axis=1)) * INV
        pert[slot] = jnp.where(is_mean, centred, raw.astype(F32)).astype(BF)

    def to_lat(src, dst, recv, other):
        return pltpu.make_async_remote_copy(
            src_ref=src, dst_ref=dst, send_sem=sem_lat, recv_sem=recv,
            device_id={"lat": other}, device_id_type=MESH,
        )

    def to_both(src, dst_down, dst_up, sem_down, sem_up):
        to_lat(src, dst_down, sem_down, upper).start()
        to_lat(src, dst_up, sem_up, lower).start()

    def landed(view, sem):
        pltpu.make_async_copy(view, view, sem).wait()

    to_both(pert.at[0], pert_down, pert_up, sem_pert.at[0], sem_pert.at[1])
    north_on = pick[6]
    south_on = pick[7]

    def build(dst, base, left, right, tiles, which, on):
        def chunk(r, carry):
            rows = pl.ds(pl.multiple_of(r * 128, 128), 128)
            prod = lax.dot_general(
                left[:, rows], right[...], (((0,), (0,)), ((), ())), preferred_element_type=F32
            )
            share = pick[which]
            tile = tiles[1, rows].astype(F32) * share + tiles[0, rows].astype(F32) * (1.0 - share)
            value = tile * prod
            if on is not None:
                value = value * on
            dst[pl.ds(pl.multiple_of(base + r * 128, 128), 128)] = value.astype(BF)
            return carry

        lax.fori_loop(0, 4, chunk, 0)

    here0, here1 = pert.at[0], pert.at[1]
    build(mat_a, 0, here0, here0, sym, 0, None)
    build(mat_a, 512, here1, here0, flip, 2, pick[5])
    build(mat_b, 0, here0, here1, taper_ref, 2, pick[5])
    build(mat_b, 512, here1, here1, sym, 1, None)
    landed(pert_up, sem_pert.at[1])
    landed(pert_down, sem_pert.at[0])
    build(mat_a, 1024, pert_up, here0, flip, 3, north_on)
    build(mat_a, 1536, pert_down, here0, taper_ref, 4, south_on)

    var = (var_ref[blocks[62]], var_ref[blocks[63]])
    keep_d = [rho1 + sig1 * (centre - v) for v in var]
    keep_y = [(1.0 + rho2 - sig2 * v) * sig1 + sig2 for v in var]

    def times(parts, mat):
        total = None
        for n, part in enumerate(parts):
            prod = jnp.dot(part, mat[pl.ds(512 * n, 512)], preferred_element_type=F32)
            total = prod if total is None else total + prod
        return total

    def stage_a(g):
        arrived(got_r, sem_r, g)
        if g == 3:
            own[2].wait()
        rows = pl.ds(8 * g, 8)
        to_both(
            got_r.at[rows, 0], dir0_down.at[rows], dir0_up.at[rows],
            sem_d0.at[g, 0], sem_d0.at[g, 1],
        )

    def stage_b(g):
        rows = pl.ds(8 * g, 8)
        landed(dir0_up.at[rows], sem_d0.at[g, 1])
        landed(dir0_down.at[rows], sem_d0.at[g, 0])
        mine = [got_r[rows, s].reshape(96, BLOCK) for s in range(2)]
        above = dir0_up[rows].reshape(96, BLOCK)
        below = dir0_down[rows].reshape(96, BLOCK)
        prods = (times((mine[0], mine[1], above, below), mat_a), times(mine, mat_b))
        for s in range(2):
            dir1[g, s] = (keep_d[s] * mine[s].astype(F32) - sig1 * prods[s]).astype(BF)
            kept[g, s] = keep_y[s] * prods[s]
        to_both(
            dir1.at[g, 0], dir1_down.at[g], dir1_up.at[g], sem_d1.at[g, 0], sem_d1.at[g, 1]
        )

    def stage_c(g):
        landed(dir1_up.at[g], sem_d1.at[g, 1])
        landed(dir1_down.at[g], sem_d1.at[g, 0])
        mine = [dir1[g, s] for s in range(2)]
        prods = (
            times((mine[0], mine[1], dir1_up[g], dir1_down[g]), mat_a), times(mine, mat_b)
        )
        for s in range(2):
            total = (kept[g, s] + sig2 * prods[s]).astype(BF)
            send_w[pl.ds(8 * g, 8), s] = total.reshape(8, 3, 4, BLOCK)
        for i in range(8 * g, 8 * g + 8):
            if i == 31:
                continue
            j = i if i < 2 or i == 30 else mirror(i)
            remote(send_w.at[i], out_ref.at[j], sem_w, i).start()

    stage_a(0)
    stage_a(1)
    stage_b(0)
    stage_a(2)
    stage_b(1)
    stage_c(0)
    stage_a(3)
    stage_b(2)
    stage_c(1)
    stage_b(3)
    stage_c(2)
    stage_c(3)
    own[3].start()
    own[3].wait()
    keep_base.wait()

    most = pl.ds(0, 31)
    landed(out_ref.at[most], sem_w)
    for sent in (send_p, send_low, send_r, send_w):
        pltpu.make_async_copy(sent.at[most], sent.at[most], sem_send).wait()
    for _ in range(2):
        pltpu.make_async_copy(pert.at[0], pert.at[0], sem_lat).wait()
        pltpu.make_async_copy(dir0_up, dir0_up, sem_lat).wait()
        pltpu.make_async_copy(dir1_up, dir1_up, sem_lat).wait()


def exchange(equivalents, innovations, variance, tapers, blocks, pick, low, high):
    chunk = (3, 4, BLOCK)
    dma = pltpu.SemaphoreType.DMA
    return pl.pallas_call(
        exchange_kernel,
        out_shape=(
            jax.ShapeDtypeStruct((32, 2) + chunk, BF),
            jax.ShapeDtypeStruct((BAND, 12, BLOCK), F32),
        ),
        in_specs=[HB, HB, HB, HB, SM, SM, SM, SM],
        out_specs=(HB, HB),
        scratch_shapes=[
            pltpu.VMEM((BAND, 12, BLOCK), F32),
            pltpu.VMEM((BAND, 12, BLOCK), F32),
            pltpu.VMEM((BAND, 12, BLOCK), F32),
            pltpu.VMEM((BAND, 1, BLOCK), F32),
            pltpu.VMEM((2, BLOCK, BLOCK), BF),
            pltpu.VMEM((32, 2) + chunk, BF),
            pltpu.VMEM((32, 4, 256), BF),
            pltpu.VMEM((32, 2) + chunk, BF),
            pltpu.VMEM((32, 2) + chunk, BF),
            pltpu.VMEM((32, 4, 256), BF),
            pltpu.VMEM((32, 2) + chunk, BF),
            pltpu.VMEM((32, 2) + chunk, BF),
            pltpu.VMEM((2, M, BLOCK), BF),
            pltpu.VMEM((M, BLOCK), BF),
            pltpu.VMEM((M, BLOCK), BF),
            pltpu.VMEM((2, BLOCK, BLOCK), F32),
            pltpu.VMEM((2, BLOCK, BLOCK), BF),
            pltpu.VMEM((4 * BLOCK, BLOCK), BF),
            pltpu.VMEM((2 * BLOCK, BLOCK), BF),
            pltpu.VMEM((32,) + chunk, BF),
            pltpu.VMEM((32,) + chunk, BF),
            pltpu.VMEM((GROUPS, 2, 96, BLOCK), BF),
            pltpu.VMEM((GROUPS, 96, BLOCK), BF),
            pltpu.VMEM((GROUPS, 96, BLOCK), BF),
            pltpu.VMEM((GROUPS, 2, 96, BLOCK), F32),
            dma,
            dma((7,)),
            dma((2, BAND)),
            dma((GROUPS,)),
            dma((GROUPS,)),
            dma((GROUPS,)),
            dma,
            dma,
            dma((2,)),
            dma((GROUPS, 2)),
            dma((GROUPS, 2)),
        ],
        compiler_params=pltpu.CompilerParams(
            collective_id=0, has_side_effects=True, vmem_limit_bytes=LIMIT
        ),
        name="exchange",
    )(equivalents, innovations, variance, tapers, blocks, pick, low, high)


STEPS = 4
PER_STEP = BAND // STEPS


def finish_kernel(base_hbm, got_hbm, where, out_hbm, base, got, out, sem_base, sem_got, sem_out):
    bands = [pl.ds(step * PER_STEP, PER_STEP) for step in range(STEPS)]
    parts = [pl.ds(8 * n, 8) for n in range(4)]
    got_loads = [
        pltpu.make_async_copy(got_hbm.at[part], got.at[part], sem_got.at[n])
        for n, part in enumerate(parts)
    ]
    base_loads = [
        pltpu.make_async_copy(base_hbm.at[part], base.at[part], sem_base.at[n])
        for n, part in enumerate(bands)
    ]
    for load in got_loads + base_loads:
        load.start()
    for load in got_loads:
        load.wait()
    copies = []
    for step in range(STEPS):
        base_loads[step].wait()
        for n in range(step * PER_STEP, (step + 1) * PER_STEP):
            entry = where[n]
            change = got[entry // 2, entry % 2].reshape(12, BLOCK).astype(F32)
            out[:, pl.ds(n * BLOCK, BLOCK)] = base[n] - change
        cols = pl.ds(step * PER_STEP * BLOCK, PER_STEP * BLOCK)
        copies.append(
            pltpu.make_async_copy(out.at[:, cols], out_hbm.at[:, cols], sem_out.at[step])
        )
        copies[-1].start()
    for copy in copies:
        copy.wait()


def finish(base, got, where):
    dma = pltpu.SemaphoreType.DMA
    return pl.pallas_call(
        finish_kernel,
        out_shape=jax.ShapeDtypeStruct((12, BAND * BLOCK), F32),
        in_specs=[HB, HB, SM],
        out_specs=HB,
        scratch_shapes=[
            pltpu.VMEM((BAND, 12, BLOCK), F32),
            pltpu.VMEM((32, 2, 3, 4, BLOCK), BF),
            pltpu.VMEM((12, BAND * BLOCK), F32),
            dma((STEPS,)),
            dma((4,)),
            dma((STEPS,)),
        ],
        compiler_params=pltpu.CompilerParams(vmem_limit_bytes=LIMIT),
        name="finish",
    )(base, got, where)


def on_device(
    equivalents, innovations, obs_var, taper_tiles, region_blocks, pair_mask, taper_index,
    eig_low, eig_high,
):
    variance = obs_var.reshape(BAND, 1, BLOCK)
    blocks, pick, where = tables(
        jnp.transpose(taper_index, (2, 0, 1)), region_blocks, pair_mask
    )
    got, base = exchange(
        equivalents, innovations, variance, taper_tiles, blocks, pick, eig_low, eig_high
    )
    return finish(base, got, where)


def solution(mesh):
    return jax.shard_map(
        on_device,
        mesh=mesh,
        in_specs=(P("mem", "lat"), P("mem", "lat"), P("lat"), P(), P(), P(), P(), P(), P()),
        out_specs=P("mem", "lat"),
        check_vma=False,
    )
```

```python
import jax
import jax.numpy as jnp
from jax import lax
from jax.experimental import pallas as pl
from jax.experimental.pallas import tpu as pltpu
from jax.sharding import PartitionSpec as P

M = 384
BLOCK = 512
BAND = 48
GROUPS = 4
LIMIT = 60 * 1024 * 1024
BF = jnp.bfloat16
F32 = jnp.float32
MESH = pl.DeviceIdType.MESH
VM = pl.BlockSpec(memory_space=pltpu.VMEM)
HB = pl.BlockSpec(memory_space=pl.ANY)
SM = pl.BlockSpec(memory_space=pltpu.SMEM)
INV = (M - 1) ** -0.5


def coefficients(lo, hi):
    low = jnp.full((1, BLOCK), lo, F32)
    high = jnp.full((1, BLOCK), hi, F32)
    centre = 0.5 * (high + low)
    half = 0.5 * (high - low)
    scale = centre / half
    q0 = 1.0 / scale
    q1 = 1.0 / (2.0 * scale - q0)
    q2 = 1.0 / (2.0 * scale - q1)
    return centre, q1 * q0, 2.0 * q1 / half, q2 * q1, 2.0 * q2 / half


def peer_of(i, z, c):
    t = i // 2
    odd = t % 2
    dz = (8 - (t + 1) // 2) * (2 * odd - 1)
    return (z + dz + 16) % 16 * 2 + (c + 1 - i % 2) % 2


def mirror(i):
    t = i // 2
    return i + 4 * (t % 2) - 2


ROOT = 12.0**0.5


def tables_kernel(index_ref, region_ref, mask_ref, blocks, pick, where, starts, low_starts):
    me = lax.axis_index("mem")
    z, c = me // 2, me % 2
    band = lax.axis_index("lat")
    lower = (band + 15) % 16

    def scan(m, totals):
        total, low_total = totals
        starts[m] = total
        low_starts[m] = low_total
        dz = (m // 2 - z + 16) % 16
        t = jnp.where(dz < 8, 15 - 2 * dz, 2 * dz - 16)
        place = 2 * (2 * t + 1 - (m + c) % 2)
        follow = jnp.minimum(total + 1, BAND - 1)
        where[follow] = place + 1
        where[total] = place
        blocks[place] = total
        blocks[place + 1] = follow
        return total + region_ref[band, m], low_total + region_ref[lower, m]

    lax.fori_loop(0, 32, scan, (jnp.int32(0), jnp.int32(0)), unroll=4)
    start = starts[me]
    second = jnp.minimum(start + 1, BAND - 1)

    def one(on):
        return jnp.where(on, 1.0, 0.0).astype(F32)

    pick[0] = one(index_ref[0, band, start] == 1)
    pick[1] = one(index_ref[0, band, second] == 1)
    pick[2] = one(index_ref[1, band, start] == 1)
    pick[3] = one(index_ref[2, band, start] == 1)
    pick[4] = one(index_ref[2, lower, low_starts[me]] == 1)
    pick[5] = one((region_ref[band, me] > 1) & (mask_ref[band, start] == 1))
    pick[6] = one(band < 15)
    pick[7] = one(band > 0)


def tables(index, regions, mask):
    return pl.pallas_call(
        tables_kernel,
        out_shape=(
            jax.ShapeDtypeStruct((64,), jnp.int32),
            jax.ShapeDtypeStruct((8,), F32),
            jax.ShapeDtypeStruct((BAND,), jnp.int32),
        ),
        in_specs=[SM, SM, SM],
        out_specs=(SM, SM, SM),
        scratch_shapes=[pltpu.SMEM((32,), jnp.int32), pltpu.SMEM((32,), jnp.int32)],
        name="tables",
    )(index, regions, mask)


def exchange_kernel(
    eq_hbm, inn_hbm, var_hbm, taper_hbm, blocks, pick, lo_ref, hi_ref,
    out_ref, base_hbm,
    base_ref,
    eq, inn, var_ref, taper_ref, send_p, send_low, send_r,
    got_p, got_low, got_r, send_w, pert, pert_up, pert_down, sym, flip, mat_a, mat_b,
    dir0_up, dir0_down, dir1, dir1_up, dir1_down, kept,
    sem_send, sem_own, sem_in, sem_p, sem_low, sem_r, sem_w, sem_lat, sem_pert, sem_d0, sem_d1,
):
    me = lax.axis_index("mem")
    z, c = me // 2, me % 2
    band = lax.axis_index("lat")
    upper = (band + 1) % 16
    lower = (band + 15) % 16

    def column(k):
        return pl.ds(pl.multiple_of(k * BLOCK, BLOCK), BLOCK)

    def fetch_block(source, target, n, k):
        return pltpu.make_async_copy(source.at[:, column(k)], target.at[k], sem_in.at[n, k])

    def start_fetch(source, target, n):
        def one(k, carry):
            fetch_block(source, target, n, k).start()
            return carry

        lax.fori_loop(0, BAND, one, 0)

    def end_fetch(source, target, n):
        def one(k, carry):
            fetch_block(source, target, n, k).wait()
            return carry

        lax.fori_loop(0, BAND, one, 0)

    barrier = pltpu.get_barrier_semaphore()

    def greet(i, carry):
        pl.semaphore_signal(barrier, inc=1, device_id={"mem": peer_of(i, z, c)}, device_id_type=MESH)
        return carry

    lax.fori_loop(0, 31, greet, 0)
    for other in (upper, lower):
        pl.semaphore_signal(barrier, inc=1, device_id={"lat": other}, device_id_type=MESH)

    centre, rho1, sig1, rho2, sig2 = coefficients(lo_ref[0], hi_ref[0])
    start_fetch(eq_hbm, eq, 0)
    start_fetch(inn_hbm, inn, 1)
    fetches = [
        pltpu.make_async_copy(taper_hbm, taper_ref, sem_own.at[4]),
        pltpu.make_async_copy(var_hbm, var_ref, sem_own.at[5]),
    ]
    for fetch in fetches:
        fetch.start()
    top = lax.broadcasted_iota(jnp.int32, (12, BLOCK), 0) == 0
    end_fetch(eq_hbm, eq, 0)

    def pack_pert(i, carry):
        lows = []
        for slot in range(2):
            values = eq[blocks[2 * i + slot]]
            total = jnp.sum(values, axis=0, keepdims=True) * (1.0 / ROOT)
            shift = (total - values[0:1]) * (1.0 / (ROOT - 1.0))
            mixed = jnp.where(top, total, (values - shift) * INV).astype(BF)
            send_p[i, slot] = mixed.reshape(3, 4, BLOCK)
            low = total - total.astype(BF).astype(F32)
            lows += [low[:, 0:256], low[:, 256:512]]
        send_low[i] = jnp.concatenate(lows, axis=0).astype(BF)
        return carry

    lax.fori_loop(0, 8, pack_pert, 0, unroll=2)
    pl.semaphore_wait(barrier, 33)

    def remote(src, dst, recv, i):
        return pltpu.make_async_remote_copy(
            src_ref=src, dst_ref=dst, send_sem=sem_send, recv_sem=recv,
            device_id={"mem": peer_of(i, z, c)}, device_id_type=MESH,
        )

    def spread(send, got, sems, low=0, high=32):
        if low == 0:
            for i in (0, 1):
                remote(send.at[i], got.at[i], sems.at[0], i).start()

        def one(i, carry):
            j = mirror(i)
            remote(send.at[i], got.at[j], sems.at[j // 8], i).start()
            return carry

        lax.fori_loop(max(low, 2), min(high, 30), one, 0)
        if high == 32:
            remote(send.at[30], got.at[30], sems.at[3], 30).start()

    def arrived(got, sems, g):
        size = 8 if g < 3 else 7
        view = got.at[pl.ds(8 * g, size)]
        pltpu.make_async_copy(view, view, sems.at[g]).wait()

    spread(send_p, got_p, sem_p, 0, 8)
    for g in range(1, GROUPS):
        lax.fori_loop(8 * g, 8 * g + 8, pack_pert, 0, unroll=2)
        spread(send_p, got_p, sem_p, 8 * g, 8 * g + 8)
    spread(send_low, got_low, sem_low)
    inv_centre = 1.0 / centre
    end_fetch(inn_hbm, inn, 1)

    def pack_rhs(i, carry):
        for slot in range(2):
            values = inn[blocks[2 * i + slot]]
            send_r[i, slot] = (values * inv_centre).astype(BF).reshape(3, 4, BLOCK)
        return carry

    lax.fori_loop(0, 32, pack_rhs, 0, unroll=2)
    spread(send_r, got_r, sem_r)
    own = [
        pltpu.make_async_copy(sent.at[31], got.at[31], sem_own.at[n])
        for n, (sent, got) in enumerate(
            ((send_p, got_p), (send_low, got_low), (send_r, got_r), (send_w, out_ref))
        )
    ]
    for copy in own[:3]:
        copy.start()
    for fetch in fetches:
        fetch.wait()
    for n in range(2):
        tile = taper_ref[n].astype(F32)
        turned = tile.T
        sym[n] = 0.5 * (tile + turned)
        flip[n] = turned.astype(BF)


    def local_part(k, carry):
        var = var_ref[k]
        keep = rho1 + sig1 * (centre - var)
        factor = 1.0 + (1.0 + rho2 - sig2 * var) * keep + sig2 * (centre - var)
        base_ref[k] = (factor * inv_centre) * inn[k]
        return carry

    lax.fori_loop(0, BAND, local_part, 0)
    keep_base = pltpu.make_async_copy(base_ref, base_hbm, sem_own.at[6])
    keep_base.start()

    for g in range(GROUPS):
        arrived(got_p, sem_p, g)
        arrived(got_low, sem_low, g)
    own[0].wait()
    own[1].wait()
    lows = got_low[...].reshape(128, 256)
    row = lax.broadcasted_iota(jnp.int32, (M, M), 0)
    col = lax.broadcasted_iota(jnp.int32, (M, M), 1)
    spot = row % 12 == 0
    centring = jnp.where(row == col, 1.0, 0.0) - 1.0 / 32.0
    centring = jnp.where(spot & (col % 12 == 0), centring, 0.0).astype(BF)
    wide_row = lax.broadcasted_iota(jnp.int32, (M, 128), 0)
    wide_col = lax.broadcasted_iota(jnp.int32, (M, 128), 1)
    part_of = jnp.where(wide_row == 12 * (wide_col // 4), 1.0, 0.0) - 1.0 / 32.0
    is_mean = lax.broadcasted_iota(jnp.int32, (M, BLOCK), 0) % 12 == 0
    for slot in range(2):
        raw = got_p[:, slot].reshape(M, BLOCK)
        halves = []
        for half in range(2):
            use = (wide_row % 12 == 0) & (wide_col % 4 == 2 * slot + half)
            weight = jnp.where(use, part_of, 0.0).astype(BF)
            halves.append(jnp.dot(weight, lows, preferred_element_type=F32))
        centred = jnp.dot(centring, raw, preferred_element_type=F32)
        centred = (centred + jnp.concatenate(halves, axis=1)) * INV
        pert[slot] = jnp.where(is_mean, centred, raw.astype(F32)).astype(BF)

    def to_lat(src, dst, recv, other):
        return pltpu.make_async_remote_copy(
            src_ref=src, dst_ref=dst, send_sem=sem_lat, recv_sem=recv,
            device_id={"lat": other}, device_id_type=MESH,
        )

    def to_both(src, dst_down, dst_up, sem_down, sem_up):
        to_lat(src, dst_down, sem_down, upper).start()
        to_lat(src, dst_up, sem_up, lower).start()

    def landed(view, sem):
        pltpu.make_async_copy(view, view, sem).wait()

    to_both(pert.at[0], pert_down, pert_up, sem_pert.at[0], sem_pert.at[1])
    north_on = pick[6]
    south_on = pick[7]

    def build(dst, base, left, right, tiles, which, on):
        def chunk(r, carry):
            rows = pl.ds(pl.multiple_of(r * 128, 128), 128)
            prod = lax.dot_general(
                left[:, rows], right[...], (((0,), (0,)), ((), ())), preferred_element_type=F32
            )
            share = pick[which]
            tile = tiles[1, rows].astype(F32) * share + tiles[0, rows].astype(F32) * (1.0 - share)
            value = tile * prod
            if on is not None:
                value = value * on
            dst[pl.ds(pl.multiple_of(base + r * 128, 128), 128)] = value.astype(BF)
            return carry

        lax.fori_loop(0, 4, chunk, 0)

    here0, here1 = pert.at[0], pert.at[1]
    build(mat_a, 0, here0, here0, sym, 0, None)
    build(mat_a, 512, here1, here0, flip, 2, pick[5])
    build(mat_b, 0, here0, here1, taper_ref, 2, pick[5])
    build(mat_b, 512, here1, here1, sym, 1, None)
    landed(pert_up, sem_pert.at[1])
    landed(pert_down, sem_pert.at[0])
    build(mat_a, 1024, pert_up, here0, flip, 3, north_on)
    build(mat_a, 1536, pert_down, here0, taper_ref, 4, south_on)

    var = (var_ref[blocks[62]], var_ref[blocks[63]])
    keep_d = [rho1 + sig1 * (centre - v) for v in var]
    keep_y = [(1.0 + rho2 - sig2 * v) * sig1 + sig2 for v in var]

    def times(parts, mat):
        total = None
        for n, part in enumerate(parts):
            prod = jnp.dot(part, mat[pl.ds(512 * n, 512)], preferred_element_type=F32)
            total = prod if total is None else total + prod
        return total

    def stage_a(g):
        arrived(got_r, sem_r, g)
        if g == 3:
            own[2].wait()
        rows = pl.ds(8 * g, 8)
        to_both(
            got_r.at[rows, 0], dir0_down.at[rows], dir0_up.at[rows],
            sem_d0.at[g, 0], sem_d0.at[g, 1],
        )

    def stage_b(g):
        rows = pl.ds(8 * g, 8)
        landed(dir0_up.at[rows], sem_d0.at[g, 1])
        landed(dir0_down.at[rows], sem_d0.at[g, 0])
        mine = [got_r[rows, s].reshape(96, BLOCK) for s in range(2)]
        above = dir0_up[rows].reshape(96, BLOCK)
        below = dir0_down[rows].reshape(96, BLOCK)
        prods = (times((mine[0], mine[1], above, below), mat_a), times(mine, mat_b))
        for s in range(2):
            dir1[g, s] = (keep_d[s] * mine[s].astype(F32) - sig1 * prods[s]).astype(BF)
            kept[g, s] = keep_y[s] * prods[s]
        to_both(
            dir1.at[g, 0], dir1_down.at[g], dir1_up.at[g], sem_d1.at[g, 0], sem_d1.at[g, 1]
        )

    def stage_c(g):
        landed(dir1_up.at[g], sem_d1.at[g, 1])
        landed(dir1_down.at[g], sem_d1.at[g, 0])
        mine = [dir1[g, s] for s in range(2)]
        prods = (
            times((mine[0], mine[1], dir1_up[g], dir1_down[g]), mat_a), times(mine, mat_b)
        )
        for s in range(2):
            total = (kept[g, s] + sig2 * prods[s]).astype(BF)
            send_w[pl.ds(8 * g, 8), s] = total.reshape(8, 3, 4, BLOCK)
        for i in range(8 * g, 8 * g + 8):
            if i == 31:
                continue
            j = i if i < 2 or i == 30 else mirror(i)
            remote(send_w.at[i], out_ref.at[j], sem_w, i).start()

    for g in (0, 1):
        stage_a(g)
        stage_b(g)
        stage_c(g)
    for stage in (stage_a, stage_b, stage_c):
        stage(2)
        stage(3)
    own[3].start()
    own[3].wait()
    keep_base.wait()

    most = pl.ds(0, 31)
    landed(out_ref.at[most], sem_w)
    for sent in (send_p, send_low, send_r, send_w):
        pltpu.make_async_copy(sent.at[most], sent.at[most], sem_send).wait()
    for _ in range(2):
        pltpu.make_async_copy(pert.at[0], pert.at[0], sem_lat).wait()
        pltpu.make_async_copy(dir0_up, dir0_up, sem_lat).wait()
        pltpu.make_async_copy(dir1_up, dir1_up, sem_lat).wait()


def exchange(equivalents, innovations, variance, tapers, blocks, pick, low, high):
    chunk = (3, 4, BLOCK)
    dma = pltpu.SemaphoreType.DMA
    return pl.pallas_call(
        exchange_kernel,
        out_shape=(
            jax.ShapeDtypeStruct((32, 2) + chunk, BF),
            jax.ShapeDtypeStruct((BAND, 12, BLOCK), F32),
        ),
        in_specs=[HB, HB, HB, HB, SM, SM, SM, SM],
        out_specs=(HB, HB),
        scratch_shapes=[
            pltpu.VMEM((BAND, 12, BLOCK), F32),
            pltpu.VMEM((BAND, 12, BLOCK), F32),
            pltpu.VMEM((BAND, 12, BLOCK), F32),
            pltpu.VMEM((BAND, 1, BLOCK), F32),
            pltpu.VMEM((2, BLOCK, BLOCK), BF),
            pltpu.VMEM((32, 2) + chunk, BF),
            pltpu.VMEM((32, 4, 256), BF),
            pltpu.VMEM((32, 2) + chunk, BF),
            pltpu.VMEM((32, 2) + chunk, BF),
            pltpu.VMEM((32, 4, 256), BF),
            pltpu.VMEM((32, 2) + chunk, BF),
            pltpu.VMEM((32, 2) + chunk, BF),
            pltpu.VMEM((2, M, BLOCK), BF),
            pltpu.VMEM((M, BLOCK), BF),
            pltpu.VMEM((M, BLOCK), BF),
            pltpu.VMEM((2, BLOCK, BLOCK), F32),
            pltpu.VMEM((2, BLOCK, BLOCK), BF),
            pltpu.VMEM((4 * BLOCK, BLOCK), BF),
            pltpu.VMEM((2 * BLOCK, BLOCK), BF),
            pltpu.VMEM((32,) + chunk, BF),
            pltpu.VMEM((32,) + chunk, BF),
            pltpu.VMEM((GROUPS, 2, 96, BLOCK), BF),
            pltpu.VMEM((GROUPS, 96, BLOCK), BF),
            pltpu.VMEM((GROUPS, 96, BLOCK), BF),
            pltpu.VMEM((GROUPS, 2, 96, BLOCK), F32),
            dma,
            dma((7,)),
            dma((2, BAND)),
            dma((GROUPS,)),
            dma((GROUPS,)),
            dma((GROUPS,)),
            dma,
            dma,
            dma((2,)),
            dma((GROUPS, 2)),
            dma((GROUPS, 2)),
        ],
        compiler_params=pltpu.CompilerParams(
            collective_id=0, has_side_effects=True, vmem_limit_bytes=LIMIT
        ),
        name="exchange",
    )(equivalents, innovations, variance, tapers, blocks, pick, low, high)


STEPS = 6
PER_STEP = BAND // STEPS


def finish_kernel(base_hbm, got_hbm, where, out_hbm, base, got, out, sem_base, sem_got, sem_out):
    bands = [pl.ds(step * PER_STEP, PER_STEP) for step in range(STEPS)]
    parts = [pl.ds(8 * n, 8) for n in range(4)]
    got_loads = [
        pltpu.make_async_copy(got_hbm.at[part], got.at[part], sem_got.at[n])
        for n, part in enumerate(parts)
    ]
    base_loads = [
        pltpu.make_async_copy(base_hbm.at[part], base.at[part], sem_base.at[n])
        for n, part in enumerate(bands)
    ]
    for load in got_loads + base_loads:
        load.start()
    for load in got_loads:
        load.wait()
    copies = []
    for step in range(STEPS):
        base_loads[step].wait()
        for n in range(step * PER_STEP, (step + 1) * PER_STEP):
            entry = where[n]
            change = got[entry // 2, entry % 2].reshape(12, BLOCK).astype(F32)
            out[:, pl.ds(n * BLOCK, BLOCK)] = base[n] - change
        cols = pl.ds(step * PER_STEP * BLOCK, PER_STEP * BLOCK)
        copies.append(
            pltpu.make_async_copy(out.at[:, cols], out_hbm.at[:, cols], sem_out.at[step])
        )
        copies[-1].start()
    for copy in copies:
        copy.wait()


def finish(base, got, where):
    dma = pltpu.SemaphoreType.DMA
    return pl.pallas_call(
        finish_kernel,
        out_shape=jax.ShapeDtypeStruct((12, BAND * BLOCK), F32),
        in_specs=[HB, HB, SM],
        out_specs=HB,
        scratch_shapes=[
            pltpu.VMEM((BAND, 12, BLOCK), F32),
            pltpu.VMEM((32, 2, 3, 4, BLOCK), BF),
            pltpu.VMEM((12, BAND * BLOCK), F32),
            dma((STEPS,)),
            dma((4,)),
            dma((STEPS,)),
        ],
        compiler_params=pltpu.CompilerParams(vmem_limit_bytes=LIMIT),
        name="finish",
    )(base, got, where)


def on_device(
    equivalents, innovations, obs_var, taper_tiles, region_blocks, pair_mask, taper_index,
    eig_low, eig_high,
):
    variance = obs_var.reshape(BAND, 1, BLOCK)
    blocks, pick, where = tables(
        jnp.transpose(taper_index, (2, 0, 1)), region_blocks, pair_mask
    )
    got, base = exchange(
        equivalents, innovations, variance, taper_tiles, blocks, pick, eig_low, eig_high
    )
    return finish(base, got, where)


def solution(mesh):
    return jax.shard_map(
        on_device,
        mesh=mesh,
        in_specs=(P("mem", "lat"), P("mem", "lat"), P("lat"), P(), P(), P(), P(), P(), P()),
        out_specs=P("mem", "lat"),
        check_vma=False,
    )
```

```python
import jax
import jax.numpy as jnp
from jax import lax
from jax.experimental import pallas as pl
from jax.experimental.pallas import tpu as pltpu
from jax.sharding import PartitionSpec as P

M = 384
BLOCK = 512
BAND = 48
GROUPS = 4
LIMIT = 60 * 1024 * 1024
BF = jnp.bfloat16
F32 = jnp.float32
MESH = pl.DeviceIdType.MESH
VM = pl.BlockSpec(memory_space=pltpu.VMEM)
HB = pl.BlockSpec(memory_space=pl.ANY)
SM = pl.BlockSpec(memory_space=pltpu.SMEM)
INV = (M - 1) ** -0.5


def coefficients(lo, hi):
    low = jnp.full((1, BLOCK), lo, F32)
    high = jnp.full((1, BLOCK), hi, F32)
    centre = 0.5 * (high + low)
    half = 0.5 * (high - low)
    scale = centre / half
    q0 = 1.0 / scale
    q1 = 1.0 / (2.0 * scale - q0)
    q2 = 1.0 / (2.0 * scale - q1)
    return centre, q1 * q0, 2.0 * q1 / half, q2 * q1, 2.0 * q2 / half


def peer_of(i, z, c):
    t = i // 2
    odd = t % 2
    dz = (8 - (t + 1) // 2) * (2 * odd - 1)
    return (z + dz + 16) % 16 * 2 + (c + 1 - i % 2) % 2


def mirror(i):
    t = i // 2
    return i + 4 * (t % 2) - 2


ROOT = 12.0**0.5


def exchange_kernel(
    eq_hbm, inn_hbm, var_hbm, taper_hbm, index_ref, region_ref, mask_ref, lo_ref, hi_ref,
    out_ref, base_hbm,
    starts, low_starts,
    base_ref,
    eq, inn, var_ref, taper_ref, send_p, send_low, send_r,
    got_p, got_low, got_r, send_w, pert, pert_up, pert_down, sym, flip, mat_a, mat_b,
    dir0_up, dir0_down, dir1, dir1_up, dir1_down, kept,
    sem_send, sem_own, sem_in, sem_p, sem_low, sem_r, sem_w, sem_lat, sem_pert, sem_d0, sem_d1,
):
    me = lax.axis_index("mem")
    z, c = me // 2, me % 2
    band = lax.axis_index("lat")
    upper = (band + 1) % 16
    lower = (band + 15) % 16

    def column(k):
        return pl.ds(pl.multiple_of(k * BLOCK, BLOCK), BLOCK)

    def fetch_block(source, target, n, k):
        return pltpu.make_async_copy(source.at[:, column(k)], target.at[k], sem_in.at[n, k])

    def start_fetch(source, target, n):
        def one(k, carry):
            fetch_block(source, target, n, k).start()
            return carry

        lax.fori_loop(0, BAND, one, 0)

    def end_fetch(source, target, n):
        def one(k, carry):
            fetch_block(source, target, n, k).wait()
            return carry

        lax.fori_loop(0, BAND, one, 0)

    barrier = pltpu.get_barrier_semaphore()

    def greet(i, carry):
        pl.semaphore_signal(barrier, inc=1, device_id={"mem": peer_of(i, z, c)}, device_id_type=MESH)
        return carry

    lax.fori_loop(0, 31, greet, 0)
    for other in (upper, lower):
        pl.semaphore_signal(barrier, inc=1, device_id={"lat": other}, device_id_type=MESH)

    centre, rho1, sig1, rho2, sig2 = coefficients(lo_ref[0], hi_ref[0])
    start_fetch(eq_hbm, eq, 0)
    start_fetch(inn_hbm, inn, 1)
    fetches = [
        pltpu.make_async_copy(taper_hbm, taper_ref, sem_own.at[4]),
        pltpu.make_async_copy(var_hbm, var_ref, sem_own.at[5]),
    ]
    for fetch in fetches:
        fetch.start()
    total = low_total = jnp.int32(0)
    for m in range(32):
        starts[m] = total
        low_starts[m] = low_total
        total = total + region_ref[band, m]
        low_total = low_total + region_ref[lower, m]

    def block_of(i, slot):
        m = peer_of(i, z, c)
        return starts[m] + slot * lax.div(region_ref[band, m], 2)

    top = lax.broadcasted_iota(jnp.int32, (12, BLOCK), 0) == 0
    end_fetch(eq_hbm, eq, 0)

    def pack_pert(i, carry):
        lows = []
        for slot in range(2):
            values = eq[block_of(i, slot)]
            total = jnp.sum(values, axis=0, keepdims=True) * (1.0 / ROOT)
            shift = (total - values[0:1]) * (1.0 / (ROOT - 1.0))
            mixed = jnp.where(top, total, (values - shift) * INV).astype(BF)
            send_p[i, slot] = mixed.reshape(3, 4, BLOCK)
            low = total - total.astype(BF).astype(F32)
            lows += [low[:, 0:256], low[:, 256:512]]
        send_low[i] = jnp.concatenate(lows, axis=0).astype(BF)
        return carry

    lax.fori_loop(0, 8, pack_pert, 0, unroll=2)
    pl.semaphore_wait(barrier, 33)

    def remote(src, dst, recv, i):
        return pltpu.make_async_remote_copy(
            src_ref=src, dst_ref=dst, send_sem=sem_send, recv_sem=recv,
            device_id={"mem": peer_of(i, z, c)}, device_id_type=MESH,
        )

    def spread(send, got, sems, low=0, high=32):
        if low == 0:
            for i in (0, 1):
                remote(send.at[i], got.at[i], sems.at[0], i).start()

        def one(i, carry):
            j = mirror(i)
            remote(send.at[i], got.at[j], sems.at[j // 8], i).start()
            return carry

        lax.fori_loop(max(low, 2), min(high, 30), one, 0)
        if high == 32:
            remote(send.at[30], got.at[30], sems.at[3], 30).start()

    def arrived(got, sems, g):
        size = 8 if g < 3 else 7
        view = got.at[pl.ds(8 * g, size)]
        pltpu.make_async_copy(view, view, sems.at[g]).wait()

    spread(send_p, got_p, sem_p, 0, 8)
    for g in range(1, GROUPS):
        lax.fori_loop(8 * g, 8 * g + 8, pack_pert, 0, unroll=2)
        spread(send_p, got_p, sem_p, 8 * g, 8 * g + 8)
    spread(send_low, got_low, sem_low)
    inv_centre = 1.0 / centre
    end_fetch(inn_hbm, inn, 1)

    def pack_rhs(i, carry):
        for slot in range(2):
            values = inn[block_of(i, slot)]
            send_r[i, slot] = (values * inv_centre).astype(BF).reshape(3, 4, BLOCK)
        return carry

    lax.fori_loop(0, 32, pack_rhs, 0, unroll=2)
    spread(send_r, got_r, sem_r)
    own = [
        pltpu.make_async_copy(sent.at[31], got.at[31], sem_own.at[n])
        for n, (sent, got) in enumerate(
            ((send_p, got_p), (send_low, got_low), (send_r, got_r), (send_w, out_ref))
        )
    ]
    for copy in own[:3]:
        copy.start()
    for fetch in fetches:
        fetch.wait()
    for n in range(2):
        tile = taper_ref[n].astype(F32)
        turned = tile.T
        sym[n] = 0.5 * (tile + turned)
        flip[n] = turned.astype(BF)


    def local_part(k, carry):
        var = var_ref[k]
        keep = rho1 + sig1 * (centre - var)
        factor = 1.0 + (1.0 + rho2 - sig2 * var) * keep + sig2 * (centre - var)
        base_ref[k] = (factor * inv_centre) * inn[k]
        return carry

    lax.fori_loop(0, BAND, local_part, 0)
    keep_base = pltpu.make_async_copy(base_ref, base_hbm, sem_own.at[6])
    keep_base.start()

    for g in range(GROUPS):
        arrived(got_p, sem_p, g)
        arrived(got_low, sem_low, g)
    own[0].wait()
    own[1].wait()
    lows = got_low[...].reshape(128, 256)
    row = lax.broadcasted_iota(jnp.int32, (M, M), 0)
    col = lax.broadcasted_iota(jnp.int32, (M, M), 1)
    spot = row % 12 == 0
    centring = jnp.where(row == col, 1.0, 0.0) - 1.0 / 32.0
    centring = jnp.where(spot & (col % 12 == 0), centring, 0.0).astype(BF)
    wide_row = lax.broadcasted_iota(jnp.int32, (M, 128), 0)
    wide_col = lax.broadcasted_iota(jnp.int32, (M, 128), 1)
    part_of = jnp.where(wide_row == 12 * (wide_col // 4), 1.0, 0.0) - 1.0 / 32.0
    is_mean = lax.broadcasted_iota(jnp.int32, (M, BLOCK), 0) % 12 == 0
    for slot in range(2):
        raw = got_p[:, slot].reshape(M, BLOCK)
        halves = []
        for half in range(2):
            use = (wide_row % 12 == 0) & (wide_col % 4 == 2 * slot + half)
            weight = jnp.where(use, part_of, 0.0).astype(BF)
            halves.append(jnp.dot(weight, lows, preferred_element_type=F32))
        centred = jnp.dot(centring, raw, preferred_element_type=F32)
        centred = (centred + jnp.concatenate(halves, axis=1)) * INV
        pert[slot] = jnp.where(is_mean, centred, raw.astype(F32)).astype(BF)

    def to_lat(src, dst, recv, other):
        return pltpu.make_async_remote_copy(
            src_ref=src, dst_ref=dst, send_sem=sem_lat, recv_sem=recv,
            device_id={"lat": other}, device_id_type=MESH,
        )

    def to_both(src, dst_down, dst_up, sem_down, sem_up):
        to_lat(src, dst_down, sem_down, upper).start()
        to_lat(src, dst_up, sem_up, lower).start()

    def landed(view, sem):
        pltpu.make_async_copy(view, view, sem).wait()

    to_both(pert.at[0], pert_down, pert_up, sem_pert.at[0], sem_pert.at[1])
    north_on = jnp.where(band < 15, 1.0, 0.0).astype(F32)
    south_on = jnp.where(band > 0, 1.0, 0.0).astype(F32)
    start = starts[me]
    double = lax.div(region_ref[band, me], 2)
    second = start + double
    east_on = (double * mask_ref[band, start]).astype(F32)
    picks = [
        index_ref[kind, row, block].astype(F32)
        for kind, row, block in (
            (0, band, start), (0, band, second), (1, band, start), (2, band, start),
            (2, lower, low_starts[me]),
        )
    ]

    def build(dst, base, left, right, tiles, which, on):
        def chunk(r, carry):
            rows = pl.ds(pl.multiple_of(r * 128, 128), 128)
            prod = lax.dot_general(
                left[:, rows], right[...], (((0,), (0,)), ((), ())), preferred_element_type=F32
            )
            share = picks[which]
            tile = tiles[1, rows].astype(F32) * share + tiles[0, rows].astype(F32) * (1.0 - share)
            value = tile * prod
            if on is not None:
                value = value * on
            dst[pl.ds(pl.multiple_of(base + r * 128, 128), 128)] = value.astype(BF)
            return carry

        lax.fori_loop(0, 4, chunk, 0)

    here0, here1 = pert.at[0], pert.at[1]
    build(mat_a, 0, here0, here0, sym, 0, None)
    build(mat_a, 512, here1, here0, flip, 2, east_on)
    build(mat_b, 0, here0, here1, taper_ref, 2, east_on)
    build(mat_b, 512, here1, here1, sym, 1, None)
    landed(pert_up, sem_pert.at[1])
    landed(pert_down, sem_pert.at[0])
    build(mat_a, 1024, pert_up, here0, flip, 3, north_on)
    build(mat_a, 1536, pert_down, here0, taper_ref, 4, south_on)

    var = (var_ref[start], var_ref[second])
    keep_d = [rho1 + sig1 * (centre - v) for v in var]
    keep_y = [(1.0 + rho2 - sig2 * v) * sig1 + sig2 for v in var]

    def times(parts, mat):
        total = None
        for n, part in enumerate(parts):
            prod = jnp.dot(part, mat[pl.ds(512 * n, 512)], preferred_element_type=F32)
            total = prod if total is None else total + prod
        return total

    def stage_a(g):
        arrived(got_r, sem_r, g)
        if g == 3:
            own[2].wait()
        rows = pl.ds(8 * g, 8)
        to_both(
            got_r.at[rows, 0], dir0_down.at[rows], dir0_up.at[rows],
            sem_d0.at[g, 0], sem_d0.at[g, 1],
        )

    def stage_b(g):
        rows = pl.ds(8 * g, 8)
        landed(dir0_up.at[rows], sem_d0.at[g, 1])
        landed(dir0_down.at[rows], sem_d0.at[g, 0])
        mine = [got_r[rows, s].reshape(96, BLOCK) for s in range(2)]
        above = dir0_up[rows].reshape(96, BLOCK)
        below = dir0_down[rows].reshape(96, BLOCK)
        prods = (times((mine[0], mine[1], above, below), mat_a), times(mine, mat_b))
        for s in range(2):
            dir1[g, s] = (keep_d[s] * mine[s].astype(F32) - sig1 * prods[s]).astype(BF)
            kept[g, s] = keep_y[s] * prods[s]
        to_both(
            dir1.at[g, 0], dir1_down.at[g], dir1_up.at[g], sem_d1.at[g, 0], sem_d1.at[g, 1]
        )

    def stage_c(g):
        landed(dir1_up.at[g], sem_d1.at[g, 1])
        landed(dir1_down.at[g], sem_d1.at[g, 0])
        mine = [dir1[g, s] for s in range(2)]
        prods = (
            times((mine[0], mine[1], dir1_up[g], dir1_down[g]), mat_a), times(mine, mat_b)
        )
        for s in range(2):
            total = (kept[g, s] + sig2 * prods[s]).astype(BF)
            send_w[pl.ds(8 * g, 8), s] = total.reshape(8, 3, 4, BLOCK)
        for i in range(8 * g, 8 * g + 8):
            if i == 31:
                continue
            j = i if i < 2 or i == 30 else mirror(i)
            remote(send_w.at[i], out_ref.at[j], sem_w, i).start()

    for g in (0, 1):
        stage_a(g)
        stage_b(g)
        stage_c(g)
    for stage in (stage_a, stage_b, stage_c):
        stage(2)
        stage(3)
    own[3].start()
    own[3].wait()
    keep_base.wait()

    most = pl.ds(0, 31)
    landed(out_ref.at[most], sem_w)
    for sent in (send_p, send_low, send_r, send_w):
        pltpu.make_async_copy(sent.at[most], sent.at[most], sem_send).wait()
    for _ in range(2):
        pltpu.make_async_copy(pert.at[0], pert.at[0], sem_lat).wait()
        pltpu.make_async_copy(dir0_up, dir0_up, sem_lat).wait()
        pltpu.make_async_copy(dir1_up, dir1_up, sem_lat).wait()


def exchange(equivalents, innovations, variance, tapers, index, regions, mask, low, high):
    chunk = (3, 4, BLOCK)
    dma = pltpu.SemaphoreType.DMA
    return pl.pallas_call(
        exchange_kernel,
        out_shape=(
            jax.ShapeDtypeStruct((32, 2) + chunk, BF),
            jax.ShapeDtypeStruct((BAND, 12, BLOCK), F32),
        ),
        in_specs=[HB, HB, HB, HB, SM, SM, SM, SM, SM],
        out_specs=(HB, HB),
        scratch_shapes=[
            pltpu.SMEM((32,), jnp.int32),
            pltpu.SMEM((32,), jnp.int32),
            pltpu.VMEM((BAND, 12, BLOCK), F32),
            pltpu.VMEM((BAND, 12, BLOCK), F32),
            pltpu.VMEM((BAND, 12, BLOCK), F32),
            pltpu.VMEM((BAND, 1, BLOCK), F32),
            pltpu.VMEM((2, BLOCK, BLOCK), BF),
            pltpu.VMEM((32, 2) + chunk, BF),
            pltpu.VMEM((32, 4, 256), BF),
            pltpu.VMEM((32, 2) + chunk, BF),
            pltpu.VMEM((32, 2) + chunk, BF),
            pltpu.VMEM((32, 4, 256), BF),
            pltpu.VMEM((32, 2) + chunk, BF),
            pltpu.VMEM((32, 2) + chunk, BF),
            pltpu.VMEM((2, M, BLOCK), BF),
            pltpu.VMEM((M, BLOCK), BF),
            pltpu.VMEM((M, BLOCK), BF),
            pltpu.VMEM((2, BLOCK, BLOCK), F32),
            pltpu.VMEM((2, BLOCK, BLOCK), BF),
            pltpu.VMEM((4 * BLOCK, BLOCK), BF),
            pltpu.VMEM((2 * BLOCK, BLOCK), BF),
            pltpu.VMEM((32,) + chunk, BF),
            pltpu.VMEM((32,) + chunk, BF),
            pltpu.VMEM((GROUPS, 2, 96, BLOCK), BF),
            pltpu.VMEM((GROUPS, 96, BLOCK), BF),
            pltpu.VMEM((GROUPS, 96, BLOCK), BF),
            pltpu.VMEM((GROUPS, 2, 96, BLOCK), F32),
            dma,
            dma((7,)),
            dma((2, BAND)),
            dma((GROUPS,)),
            dma((GROUPS,)),
            dma((GROUPS,)),
            dma,
            dma,
            dma((2,)),
            dma((GROUPS, 2)),
            dma((GROUPS, 2)),
        ],
        compiler_params=pltpu.CompilerParams(
            collective_id=0, has_side_effects=True, vmem_limit_bytes=LIMIT
        ),
        name="exchange",
    )(equivalents, innovations, variance, tapers, index, regions, mask, low, high)


STEPS = 6
PER_STEP = BAND // STEPS


def finish_kernel(
    base_hbm, got_hbm, region_ref, out_hbm, base, got, out, where, sem_base, sem_got, sem_out
):
    bands = [pl.ds(step * PER_STEP, PER_STEP) for step in range(STEPS)]
    parts = [pl.ds(8 * n, 8) for n in range(4)]
    got_loads = [
        pltpu.make_async_copy(got_hbm.at[part], got.at[part], sem_got.at[n])
        for n, part in enumerate(parts)
    ]
    base_loads = [
        pltpu.make_async_copy(base_hbm.at[part], base.at[part], sem_base.at[n])
        for n, part in enumerate(bands)
    ]
    for load in got_loads + base_loads:
        load.start()
    me = lax.axis_index("mem")
    z, c = me // 2, me % 2
    band = lax.axis_index("lat")

    def scan(m, total):
        dz = (m // 2 - z + 16) % 16
        t = jnp.where(dz < 8, 15 - 2 * dz, 2 * dz - 16)
        place = 2 * (2 * t + 1 - (m + c) % 2)
        where[jnp.minimum(total + 1, BAND - 1)] = place + 1
        where[total] = place
        return total + region_ref[band, m]

    lax.fori_loop(0, 32, scan, jnp.int32(0), unroll=4)
    for load in got_loads:
        load.wait()
    copies = []
    for step in range(STEPS):
        base_loads[step].wait()
        for n in range(step * PER_STEP, (step + 1) * PER_STEP):
            entry = where[n]
            change = got[entry // 2, entry % 2].reshape(12, BLOCK).astype(F32)
            out[:, pl.ds(n * BLOCK, BLOCK)] = base[n] - change
        cols = pl.ds(step * PER_STEP * BLOCK, PER_STEP * BLOCK)
        copies.append(
            pltpu.make_async_copy(out.at[:, cols], out_hbm.at[:, cols], sem_out.at[step])
        )
        copies[-1].start()
    for copy in copies:
        copy.wait()


def finish(base, got, regions):
    dma = pltpu.SemaphoreType.DMA
    return pl.pallas_call(
        finish_kernel,
        out_shape=jax.ShapeDtypeStruct((12, BAND * BLOCK), F32),
        in_specs=[HB, HB, SM],
        out_specs=HB,
        scratch_shapes=[
            pltpu.VMEM((BAND, 12, BLOCK), F32),
            pltpu.VMEM((32, 2, 3, 4, BLOCK), BF),
            pltpu.VMEM((12, BAND * BLOCK), F32),
            pltpu.SMEM((BAND,), jnp.int32),
            dma((STEPS,)),
            dma((4,)),
            dma((STEPS,)),
        ],
        compiler_params=pltpu.CompilerParams(vmem_limit_bytes=LIMIT),
        name="finish",
    )(base, got, regions)


def on_device(
    equivalents, innovations, obs_var, taper_tiles, region_blocks, pair_mask, taper_index,
    eig_low, eig_high,
):
    variance = obs_var.reshape(BAND, 1, BLOCK)
    got, base = exchange(
        equivalents, innovations, variance, taper_tiles, jnp.transpose(taper_index, (2, 0, 1)),
        region_blocks, pair_mask, eig_low, eig_high,
    )
    return finish(base, got, region_blocks)


def solution(mesh):
    return jax.shard_map(
        on_device,
        mesh=mesh,
        in_specs=(P("mem", "lat"), P("mem", "lat"), P("lat"), P(), P(), P(), P(), P(), P()),
        out_specs=P("mem", "lat"),
        check_vma=False,
    )
```

```python
import jax
import jax.numpy as jnp
from jax import lax
from jax.experimental import pallas as pl
from jax.experimental.pallas import tpu as pltpu
from jax.sharding import PartitionSpec as P

M = 384
BLOCK = 512
BAND = 48
GROUPS = 4
LIMIT = 60 * 1024 * 1024
BF = jnp.bfloat16
F32 = jnp.float32
MESH = pl.DeviceIdType.MESH
VM = pl.BlockSpec(memory_space=pltpu.VMEM)
HB = pl.BlockSpec(memory_space=pl.ANY)
SM = pl.BlockSpec(memory_space=pltpu.SMEM)
INV = (M - 1) ** -0.5


def coefficients(lo, hi):
    low = jnp.full((1, BLOCK), lo, F32)
    high = jnp.full((1, BLOCK), hi, F32)
    centre = 0.5 * (high + low)
    half = 0.5 * (high - low)
    scale = centre / half
    q0 = 1.0 / scale
    q1 = 1.0 / (2.0 * scale - q0)
    q2 = 1.0 / (2.0 * scale - q1)
    return centre, q1 * q0, 2.0 * q1 / half, q2 * q1, 2.0 * q2 / half


def peer_of(i, z, c):
    t = i // 2
    odd = t % 2
    dz = (8 - (t + 1) // 2) * (2 * odd - 1)
    return lax.rem(z + dz + 16, 16) * 2 + lax.rem(c + 1 - i % 2, 2)


def mirror(i):
    t = i // 2
    return i + 4 * (t % 2) - 2


ROOT = 12.0**0.5


def exchange_kernel(
    eq_hbm, inn_hbm, var_hbm, taper_hbm, index_ref, region_ref, mask_ref, lo_ref, hi_ref,
    out_ref, base_hbm,
    starts, low_starts,
    base_ref,
    eq, inn, var_ref, taper_ref, send_p, send_low, send_r,
    got_p, got_low, got_r, send_w, pert, pert_up, pert_down, sym, flip, mat_a, mat_b,
    dir0_up, dir0_down, dir1, dir1_up, dir1_down, kept,
    sem_send, sem_own, sem_in, sem_p, sem_low, sem_r, sem_w, sem_lat, sem_pert, sem_d0, sem_d1,
):
    me = lax.axis_index("mem")
    z, c = me // 2, me % 2
    band = lax.axis_index("lat")
    upper = (band + 1) % 16
    lower = (band + 15) % 16

    def column(k):
        return pl.ds(pl.multiple_of(k * BLOCK, BLOCK), BLOCK)

    def fetch_block(source, target, n, k):
        return pltpu.make_async_copy(source.at[:, column(k)], target.at[k], sem_in.at[n, k])

    def start_fetch(source, target, n):
        def one(k, carry):
            fetch_block(source, target, n, k).start()
            return carry

        lax.fori_loop(0, BAND, one, 0)

    def end_fetch(source, target, n):
        def one(k, carry):
            fetch_block(source, target, n, k).wait()
            return carry

        lax.fori_loop(0, BAND, one, 0)

    barrier = pltpu.get_barrier_semaphore()

    for i in range(31):
        t = i // 2
        dz = (8 - (t + 1) // 2) * (2 * (t % 2) - 1)
        other = lax.rem(z + (dz + 16), 16) * 2 + (c if i % 2 else 1 - c)
        pl.semaphore_signal(barrier, inc=1, device_id={"mem": other}, device_id_type=MESH)
    for other in (upper, lower):
        pl.semaphore_signal(barrier, inc=1, device_id={"lat": other}, device_id_type=MESH)

    centre, rho1, sig1, rho2, sig2 = coefficients(lo_ref[0], hi_ref[0])
    start_fetch(eq_hbm, eq, 0)
    fetches = [
        pltpu.make_async_copy(taper_hbm, taper_ref, sem_own.at[4]),
        pltpu.make_async_copy(var_hbm, var_ref, sem_own.at[5]),
    ]
    total = low_total = jnp.int32(0)
    for m in range(32):
        starts[m] = total
        low_starts[m] = low_total
        total = total + region_ref[band, m]
        low_total = low_total + region_ref[lower, m]

    def block_of(i, slot):
        m = peer_of(i, z, c)
        return starts[m] + slot * lax.div(region_ref[band, m], 2)

    top = lax.broadcasted_iota(jnp.int32, (12, BLOCK), 0) == 0
    end_fetch(eq_hbm, eq, 0)

    def pack_pert(i, carry):
        lows = []
        for slot in range(2):
            values = eq[block_of(i, slot)]
            total = jnp.sum(values, axis=0, keepdims=True) * (1.0 / ROOT)
            shift = (total - values[0:1]) * (1.0 / (ROOT - 1.0))
            mixed = jnp.where(top, total, (values - shift) * INV).astype(BF)
            send_p[i, slot] = mixed.reshape(3, 4, BLOCK)
            low = total - total.astype(BF).astype(F32)
            lows += [low[:, 0:256], low[:, 256:512]]
        send_low[i] = jnp.concatenate(lows, axis=0).astype(BF)
        return carry

    lax.fori_loop(0, 8, pack_pert, 0, unroll=2)
    pl.semaphore_wait(barrier, 33)

    def remote(src, dst, recv, i):
        return pltpu.make_async_remote_copy(
            src_ref=src, dst_ref=dst, send_sem=sem_send, recv_sem=recv,
            device_id={"mem": peer_of(i, z, c)}, device_id_type=MESH,
        )

    def spread(send, got, sems, low=0, high=32):
        if low == 0:
            for i in (0, 1):
                remote(send.at[i], got.at[i], sems.at[0], i).start()

        def one(i, carry):
            j = mirror(i)
            remote(send.at[i], got.at[j], sems.at[j // 8], i).start()
            return carry

        lax.fori_loop(max(low, 2), min(high, 30), one, 0)
        if high == 32:
            remote(send.at[30], got.at[30], sems.at[3], 30).start()

    def arrived(got, sems, g):
        size = 8 if g < 3 else 7
        view = got.at[pl.ds(8 * g, size)]
        pltpu.make_async_copy(view, view, sems.at[g]).wait()

    spread(send_p, got_p, sem_p, 0, 8)
    start_fetch(inn_hbm, inn, 1)
    for fetch in fetches:
        fetch.start()
    for g in range(1, GROUPS):
        lax.fori_loop(8 * g, 8 * g + 8, pack_pert, 0, unroll=2)
        spread(send_p, got_p, sem_p, 8 * g, 8 * g + 8)
    spread(send_low, got_low, sem_low)
    inv_centre = 1.0 / centre
    end_fetch(inn_hbm, inn, 1)

    def pack_rhs(i, carry):
        for slot in range(2):
            values = inn[block_of(i, slot)]
            send_r[i, slot] = (values * inv_centre).astype(BF).reshape(3, 4, BLOCK)
        return carry

    lax.fori_loop(0, 32, pack_rhs, 0, unroll=2)
    spread(send_r, got_r, sem_r)
    own = [
        pltpu.make_async_copy(sent.at[31], got.at[31], sem_own.at[n])
        for n, (sent, got) in enumerate(
            ((send_p, got_p), (send_low, got_low), (send_r, got_r), (send_w, out_ref))
        )
    ]
    for copy in own[:3]:
        copy.start()
    for fetch in fetches:
        fetch.wait()
    for n in range(2):
        tile = taper_ref[n].astype(F32)
        turned = tile.T
        sym[n] = 0.5 * (tile + turned)
        flip[n] = turned.astype(BF)


    def local_part(k, carry):
        var = var_ref[k]
        keep = rho1 + sig1 * (centre - var)
        factor = 1.0 + (1.0 + rho2 - sig2 * var) * keep + sig2 * (centre - var)
        base_ref[k] = (factor * inv_centre) * inn[k]
        return carry

    lax.fori_loop(0, BAND, local_part, 0)
    keep_base = pltpu.make_async_copy(base_ref, base_hbm, sem_own.at[6])
    keep_base.start()

    for g in range(GROUPS):
        arrived(got_p, sem_p, g)
        arrived(got_low, sem_low, g)
    own[0].wait()
    own[1].wait()
    lows = got_low[...].reshape(128, 256)
    row = lax.broadcasted_iota(jnp.int32, (M, M), 0)
    col = lax.broadcasted_iota(jnp.int32, (M, M), 1)
    spot = row % 12 == 0
    centring = jnp.where(row == col, 1.0, 0.0) - 1.0 / 32.0
    centring = jnp.where(spot & (col % 12 == 0), centring, 0.0).astype(BF)
    wide_row = lax.broadcasted_iota(jnp.int32, (M, 128), 0)
    wide_col = lax.broadcasted_iota(jnp.int32, (M, 128), 1)
    part_of = jnp.where(wide_row == 12 * (wide_col // 4), 1.0, 0.0) - 1.0 / 32.0
    is_mean = lax.broadcasted_iota(jnp.int32, (M, BLOCK), 0) % 12 == 0
    for slot in range(2):
        raw = got_p[:, slot].reshape(M, BLOCK)
        halves = []
        for half in range(2):
            use = (wide_row % 12 == 0) & (wide_col % 4 == 2 * slot + half)
            weight = jnp.where(use, part_of, 0.0).astype(BF)
            halves.append(jnp.dot(weight, lows, preferred_element_type=F32))
        centred = jnp.dot(centring, raw, preferred_element_type=F32)
        centred = (centred + jnp.concatenate(halves, axis=1)) * INV
        pert[slot] = jnp.where(is_mean, centred, raw.astype(F32)).astype(BF)

    def to_lat(src, dst, recv, other):
        return pltpu.make_async_remote_copy(
            src_ref=src, dst_ref=dst, send_sem=sem_lat, recv_sem=recv,
            device_id={"lat": other}, device_id_type=MESH,
        )

    def to_both(src, dst_down, dst_up, sem_down, sem_up):
        to_lat(src, dst_down, sem_down, upper).start()
        to_lat(src, dst_up, sem_up, lower).start()

    def landed(view, sem):
        pltpu.make_async_copy(view, view, sem).wait()

    to_both(pert.at[0], pert_down, pert_up, sem_pert.at[0], sem_pert.at[1])
    north_on = jnp.where(band < 15, 1.0, 0.0).astype(F32)
    south_on = jnp.where(band > 0, 1.0, 0.0).astype(F32)
    start = starts[me]
    double = lax.div(region_ref[band, me], 2)
    second = start + double
    east_on = (double * mask_ref[band, start]).astype(F32)
    picks = [
        index_ref[kind, row, block].astype(F32)
        for kind, row, block in (
            (0, band, start), (0, band, second), (1, band, start), (2, band, start),
            (2, lower, low_starts[me]),
        )
    ]

    def build(dst, base, left, right, tiles, which, on):
        def chunk(r, carry):
            rows = pl.ds(pl.multiple_of(r * 128, 128), 128)
            prod = lax.dot_general(
                left[:, rows], right[...], (((0,), (0,)), ((), ())), preferred_element_type=F32
            )
            share = picks[which]
            tile = tiles[1, rows].astype(F32) * share + tiles[0, rows].astype(F32) * (1.0 - share)
            value = tile * prod
            if on is not None:
                value = value * on
            dst[pl.ds(pl.multiple_of(base + r * 128, 128), 128)] = value.astype(BF)
            return carry

        lax.fori_loop(0, 4, chunk, 0)

    here0, here1 = pert.at[0], pert.at[1]
    build(mat_a, 0, here0, here0, sym, 0, None)
    build(mat_a, 512, here1, here0, flip, 2, east_on)
    build(mat_b, 0, here0, here1, taper_ref, 2, east_on)
    build(mat_b, 512, here1, here1, sym, 1, None)
    landed(pert_up, sem_pert.at[1])
    landed(pert_down, sem_pert.at[0])
    build(mat_a, 1024, pert_up, here0, flip, 3, north_on)
    build(mat_a, 1536, pert_down, here0, taper_ref, 4, south_on)

    var = (var_ref[start], var_ref[second])
    keep_d = [rho1 + sig1 * (centre - v) for v in var]
    keep_y = [(1.0 + rho2 - sig2 * v) * sig1 + sig2 for v in var]

    def times(parts, mat):
        total = None
        for n, part in enumerate(parts):
            prod = jnp.dot(part, mat[pl.ds(512 * n, 512)], preferred_element_type=F32)
            total = prod if total is None else total + prod
        return total

    def stage_a(g):
        arrived(got_r, sem_r, g)
        if g == 3:
            own[2].wait()
        rows = pl.ds(8 * g, 8)
        to_both(
            got_r.at[rows, 0], dir0_down.at[rows], dir0_up.at[rows],
            sem_d0.at[g, 0], sem_d0.at[g, 1],
        )

    def stage_b(g):
        rows = pl.ds(8 * g, 8)
        landed(dir0_up.at[rows], sem_d0.at[g, 1])
        landed(dir0_down.at[rows], sem_d0.at[g, 0])
        mine = [got_r[rows, s].reshape(96, BLOCK) for s in range(2)]
        above = dir0_up[rows].reshape(96, BLOCK)
        below = dir0_down[rows].reshape(96, BLOCK)
        prods = (times((mine[0], mine[1], above, below), mat_a), times(mine, mat_b))
        for s in range(2):
            dir1[g, s] = (keep_d[s] * mine[s].astype(F32) - sig1 * prods[s]).astype(BF)
            kept[g, s] = keep_y[s] * prods[s]
        to_both(
            dir1.at[g, 0], dir1_down.at[g], dir1_up.at[g], sem_d1.at[g, 0], sem_d1.at[g, 1]
        )

    def stage_c(g):
        landed(dir1_up.at[g], sem_d1.at[g, 1])
        landed(dir1_down.at[g], sem_d1.at[g, 0])
        mine = [dir1[g, s] for s in range(2)]
        prods = (
            times((mine[0], mine[1], dir1_up[g], dir1_down[g]), mat_a), times(mine, mat_b)
        )
        for s in range(2):
            total = (kept[g, s] + sig2 * prods[s]).astype(BF)
            send_w[pl.ds(8 * g, 8), s] = total.reshape(8, 3, 4, BLOCK)
        for i in range(8 * g, 8 * g + 8):
            if i == 31:
                continue
            j = i if i < 2 or i == 30 else mirror(i)
            remote(send_w.at[i], out_ref.at[j], sem_w, i).start()

    for g in (0, 1):
        stage_a(g)
        stage_b(g)
        stage_c(g)
    for stage in (stage_a, stage_b, stage_c):
        stage(2)
        stage(3)
    own[3].start()
    own[3].wait()
    keep_base.wait()

    most = pl.ds(0, 31)
    landed(out_ref.at[most], sem_w)
    for sent in (send_p, send_low, send_r, send_w):
        pltpu.make_async_copy(sent.at[most], sent.at[most], sem_send).wait()
    for _ in range(2):
        pltpu.make_async_copy(pert.at[0], pert.at[0], sem_lat).wait()
        pltpu.make_async_copy(dir0_up, dir0_up, sem_lat).wait()
        pltpu.make_async_copy(dir1_up, dir1_up, sem_lat).wait()


def exchange(equivalents, innovations, variance, tapers, index, regions, mask, low, high):
    chunk = (3, 4, BLOCK)
    dma = pltpu.SemaphoreType.DMA
    return pl.pallas_call(
        exchange_kernel,
        out_shape=(
            jax.ShapeDtypeStruct((32, 2) + chunk, BF),
            jax.ShapeDtypeStruct((BAND, 12, BLOCK), F32),
        ),
        in_specs=[HB, HB, HB, HB, SM, SM, SM, SM, SM],
        out_specs=(HB, HB),
        scratch_shapes=[
            pltpu.SMEM((32,), jnp.int32),
            pltpu.SMEM((32,), jnp.int32),
            pltpu.VMEM((BAND, 12, BLOCK), F32),
            pltpu.VMEM((BAND, 12, BLOCK), F32),
            pltpu.VMEM((BAND, 12, BLOCK), F32),
            pltpu.VMEM((BAND, 1, BLOCK), F32),
            pltpu.VMEM((2, BLOCK, BLOCK), BF),
            pltpu.VMEM((32, 2) + chunk, BF),
            pltpu.VMEM((32, 4, 256), BF),
            pltpu.VMEM((32, 2) + chunk, BF),
            pltpu.VMEM((32, 2) + chunk, BF),
            pltpu.VMEM((32, 4, 256), BF),
            pltpu.VMEM((32, 2) + chunk, BF),
            pltpu.VMEM((32, 2) + chunk, BF),
            pltpu.VMEM((2, M, BLOCK), BF),
            pltpu.VMEM((M, BLOCK), BF),
            pltpu.VMEM((M, BLOCK), BF),
            pltpu.VMEM((2, BLOCK, BLOCK), F32),
            pltpu.VMEM((2, BLOCK, BLOCK), BF),
            pltpu.VMEM((4 * BLOCK, BLOCK), BF),
            pltpu.VMEM((2 * BLOCK, BLOCK), BF),
            pltpu.VMEM((32,) + chunk, BF),
            pltpu.VMEM((32,) + chunk, BF),
            pltpu.VMEM((GROUPS, 2, 96, BLOCK), BF),
            pltpu.VMEM((GROUPS, 96, BLOCK), BF),
            pltpu.VMEM((GROUPS, 96, BLOCK), BF),
            pltpu.VMEM((GROUPS, 2, 96, BLOCK), F32),
            dma,
            dma((7,)),
            dma((2, BAND)),
            dma((GROUPS,)),
            dma((GROUPS,)),
            dma((GROUPS,)),
            dma,
            dma,
            dma((2,)),
            dma((GROUPS, 2)),
            dma((GROUPS, 2)),
        ],
        compiler_params=pltpu.CompilerParams(
            collective_id=0, has_side_effects=True, vmem_limit_bytes=LIMIT
        ),
        name="exchange",
    )(equivalents, innovations, variance, tapers, index, regions, mask, low, high)


STEPS = 6
PER_STEP = BAND // STEPS


def finish_kernel(
    base_hbm, got_hbm, region_ref, out_hbm, base, got, out, where, sem_base, sem_got, sem_out
):
    bands = [pl.ds(step * PER_STEP, PER_STEP) for step in range(STEPS)]
    parts = [pl.ds(8 * n, 8) for n in range(4)]
    got_loads = [
        pltpu.make_async_copy(got_hbm.at[part], got.at[part], sem_got.at[n])
        for n, part in enumerate(parts)
    ]
    base_loads = [
        pltpu.make_async_copy(base_hbm.at[part], base.at[part], sem_base.at[n])
        for n, part in enumerate(bands)
    ]
    for load in got_loads + base_loads:
        load.start()
    me = lax.axis_index("mem")
    z, c = me // 2, me % 2
    band = lax.axis_index("lat")

    def scan(m, total):
        dz = (m // 2 - z + 16) % 16
        t = jnp.where(dz < 8, 15 - 2 * dz, 2 * dz - 16)
        place = 2 * (2 * t + 1 - (m + c) % 2)
        where[jnp.minimum(total + 1, BAND - 1)] = place + 1
        where[total] = place
        return total + region_ref[band, m]

    lax.fori_loop(0, 32, scan, jnp.int32(0), unroll=4)
    for load in got_loads:
        load.wait()
    copies = []
    for step in range(STEPS):
        base_loads[step].wait()
        for n in range(step * PER_STEP, (step + 1) * PER_STEP):
            entry = where[n]
            change = got[entry // 2, entry % 2].reshape(12, BLOCK).astype(F32)
            out[:, pl.ds(n * BLOCK, BLOCK)] = base[n] - change
        cols = pl.ds(step * PER_STEP * BLOCK, PER_STEP * BLOCK)
        copies.append(
            pltpu.make_async_copy(out.at[:, cols], out_hbm.at[:, cols], sem_out.at[step])
        )
        copies[-1].start()
    for copy in copies:
        copy.wait()


def finish(base, got, regions):
    dma = pltpu.SemaphoreType.DMA
    return pl.pallas_call(
        finish_kernel,
        out_shape=jax.ShapeDtypeStruct((12, BAND * BLOCK), F32),
        in_specs=[HB, HB, SM],
        out_specs=HB,
        scratch_shapes=[
            pltpu.VMEM((BAND, 12, BLOCK), F32),
            pltpu.VMEM((32, 2, 3, 4, BLOCK), BF),
            pltpu.VMEM((12, BAND * BLOCK), F32),
            pltpu.SMEM((BAND,), jnp.int32),
            dma((STEPS,)),
            dma((4,)),
            dma((STEPS,)),
        ],
        compiler_params=pltpu.CompilerParams(vmem_limit_bytes=LIMIT),
        name="finish",
    )(base, got, regions)


def on_device(
    equivalents, innovations, obs_var, taper_tiles, region_blocks, pair_mask, taper_index,
    eig_low, eig_high,
):
    variance = obs_var.reshape(BAND, 1, BLOCK)
    got, base = exchange(
        equivalents, innovations, variance, taper_tiles, jnp.transpose(taper_index, (2, 0, 1)),
        region_blocks, pair_mask, eig_low, eig_high,
    )
    return finish(base, got, region_blocks)


def solution(mesh):
    return jax.shard_map(
        on_device,
        mesh=mesh,
        in_specs=(P("mem", "lat"), P("mem", "lat"), P("lat"), P(), P(), P(), P(), P(), P()),
        out_specs=P("mem", "lat"),
        check_vma=False,
    )
```
